256 devices in a mesh: row: 8 (over z_lo, x), col: 32 (over z_hi, y, core).
Axes of the slice: x: 4, y: 4, z: 8 (z_hi: 4, z_lo: 2; z = z_hi * 2 + z_lo), core: 2. Of those that a mesh axis runs over, the one named last changes fastest.
Arguments:
- wave_field: float32 [64, 128, 64, 128], P(None, 'col', 'row'), may hold values from -6 to 6
- medium_term: float32 [128, 64, 128], P('col', 'row'), may hold values from 0.5 to 4
- node_flux: float32 [64, 32, 8, 384], P(None, 'col', 'row'), may hold values from -6 to 6
- node_cell: int32 [32, 8, 384], P('col', 'row'), may hold values from 0 to 4095
- block_target: int32 [32, 8, 32], P('col', 'row'), may hold values from 0 to 31, as said below
- boundary_matrix: bfloat16 [2, 4096, 98304], P(None, 'row', 'col'), may hold values from -0.0390625 to 0.0390625
Outputs:
- volume_image: float32 [64, 128, 64, 128], P(None, 'col', 'row')
- boundary_image: float32 [4096, 64], P(('row', 'col'))
The draws below stay inside these ranges and needn't reach their ends.
Inputs may be any that keep to these rules, and one draw needn't show every extreme that they name: For every brick (c, r), block_target[c, r, :] is a permutation of the 32 column blocks.
All inputs are finite; a program needn't handle non-finite values.
Results may differ from the reference program's by a relative error of at most 0.0029.
Values may be sent and summed in bfloat16 or wider, within the bound.
A program may use at most 64 MiB of HBM per device.

```python
import math
import jax
import jax.numpy as jnp
from jax import lax

ANGLES = 32
COMP = 64
BRICK_X = 4
BRICK_Y = 8
BRICK_Z = 128
NODES_DEV = 384
SLAB_DEV = 512
COL_BLOCKS = 32
ROW_BLOCKS = 8
SLOT_NODES = 12
COL_NODES = 3072
NODES = 98304
SLAB_ROWS = 4096
GRID_X = 128
GRID_Y = 64
GRID_Z = 128


def draw_block_target(key, part):
    key_list = jax.random.split(jax.random.fold_in(key, 11), COL_BLOCKS * ROW_BLOCKS)
    orders = jax.vmap(lambda single: jax.random.permutation(single, COL_BLOCKS))(key_list)
    return orders.reshape(COL_BLOCKS, ROW_BLOCKS, COL_BLOCKS).astype(jnp.int32)


def with_ends(array, own_key, smallest, high):
    longest = array.shape.index(max(array.shape))
    spots = []
    for shift in (0, 1):
        where = [jax.random.randint(jax.random.fold_in(own_key, axis), (), 0, length) for axis, length in enumerate(array.shape)]
        where[longest] = (where[longest] + shift) % array.shape[longest]
        spots.append(tuple(where))
    return array.at[spots[0]].set(smallest).at[spots[1]].set(high)


def strengthened(result, own_key, source, target, blocks, factor):
    owner, partner = [(jnp.arange(result.shape[axis_at]) // (result.shape[axis_at] // blocks)).reshape([-1 if axis == axis_at else 1 for axis in range(result.ndim)]) for axis_at in (source, target)]
    chosen = jax.random.permutation(own_key, blocks)[partner]
    strong = (owner == chosen) | (owner == (partner + blocks // 2) % blocks)
    return jnp.where(strong, factor * result, result)


def steps_of(rng, extent, cuts, low, largest):
    level, own = 1.0, jax.random.fold_in(rng, 6)
    for axis_at, blocks in cuts:
        steps = jnp.exp(jax.random.uniform(jax.random.fold_in(own, axis_at), (blocks,), jnp.float32, low / len(cuts), largest / len(cuts)))
        level = level * jnp.repeat(steps, extent[axis_at] // blocks).reshape([-1 if axis == axis_at else 1 for axis in range(len(extent))])
    return level


def centred(stream_key, dims, scale, reach, pieces=(), kind=jnp.bfloat16):
    drawn = jax.random.normal(stream_key, dims, jnp.float32) * scale
    if len(pieces) > 0:
        drawn = steps_of(stream_key, dims, pieces, -0.22, 0.18) * drawn
    return jnp.clip(drawn, min=-reach, max=reach).astype(kind)


def gaussian_with(stream_key, shape, deviation, limit, cuts, heavy, kind=jnp.bfloat16):
    drawn = deviation * jax.random.normal(stream_key, shape, jnp.float32)
    if cuts:
        drawn = drawn * steps_of(stream_key, shape, cuts, -0.22, 0.18)
    return jnp.clip(strengthened(drawn, jax.random.fold_in(stream_key, 3), *heavy), -limit, limit).astype(kind)


def setup_inputs(seed: int = 0) -> dict:
    streams_of = jax.random.split(jax.random.key(seed), 7)
    return {
        "wave_field": centred(streams_of[0], (COMP, GRID_X, GRID_Y, GRID_Z), 1.0, 6.0, ((1, 32), (2, 8)), jnp.float32),
        "medium_term": jnp.clip(jnp.exp(math.log(4.0) - 2.0794415 * jax.random.uniform(streams_of[1], (GRID_X, GRID_Y, GRID_Z), jnp.float32) ** steps_of(streams_of[1], (GRID_X, GRID_Y, GRID_Z), ((0, 32), (1, 8)), -0.2, 0.2)), 0.5, 4.0),
        "node_flux": centred(streams_of[2], (COMP, COL_BLOCKS, ROW_BLOCKS, NODES_DEV), 1.0, 6.0, ((1, 32), (2, 8)), jnp.float32),
        "node_cell": with_ends(jax.random.randint(streams_of[3], (COL_BLOCKS, ROW_BLOCKS, NODES_DEV), 0, BRICK_X * BRICK_Y * BRICK_Z), jax.random.fold_in(streams_of[3], 1), 0, (BRICK_X * BRICK_Y * BRICK_Z) - 1).astype(jnp.int32),
        "block_target": draw_block_target(jax.random.fold_in(streams_of[6], 71), 0),
        "boundary_matrix": gaussian_with(streams_of[5], (2, SLAB_ROWS, NODES), NODES ** -0.5, 0.0390625, ((1, 8), (2, 32)), (2, 1, 32, 2.75)),
    }


stiff_weights = (8.0 / 3.0, 0.0, -1.0 / 6.0, -1.0 / 12.0)
mass_weights = (8.0 / 27.0, 4.0 / 27.0, 2.0 / 27.0, 1.0 / 27.0)


def apply_volume(values, medium_term):
    padded = jnp.pad(values, 1)
    width_x, width_y, depth_cells = values.shape
    stiffness = jnp.zeros_like(values)
    mass_sum = jnp.zeros_like(values)
    for offset_x in (-1, 0, 1):
        for offset_y in (-1, 0, 1):
            for offset_z in (-1, 0, 1):
                shifted = padded[1 + offset_x:1 + offset_x + width_x, 1 + offset_y:1 + offset_y + width_y, 1 + offset_z:1 + offset_z + depth_cells]
                distance = abs(offset_x) + abs(offset_y) + abs(offset_z)
                stiffness = stiffness + stiff_weights[distance] * shifted
                mass_sum = mass_sum + mass_weights[distance] * shifted
    return stiffness - medium_term * mass_sum


def reference(wave_field, medium_term, node_flux, node_cell, block_target, boundary_matrix):
    volume_image = lax.map(lambda single: apply_volume(single, medium_term), wave_field)
    brick_x = jnp.arange(COL_BLOCKS, dtype=jnp.int32)[:, None, None]
    brick_y = jnp.arange(ROW_BLOCKS, dtype=jnp.int32)[None, :, None]
    local_x = node_cell // (BRICK_Y * BRICK_Z)
    local_y = (node_cell // BRICK_Z) % BRICK_Y
    local_z = node_cell % BRICK_Z
    global_index = ((brick_x * BRICK_X + local_x) * GRID_Y + brick_y * BRICK_Y + local_y) * GRID_Z + local_z
    global_index = global_index.reshape(-1).astype(jnp.int32)
    flat_image = volume_image.reshape(COMP, -1)
    flat_image = flat_image.at[:, global_index].add(-node_flux.reshape(COMP, -1))
    volume_image = flat_image.reshape(COMP, GRID_X, GRID_Y, GRID_Z)
    flat_field = wave_field.reshape(COMP, -1)
    traces = flat_field[:, global_index].astype(jnp.bfloat16)
    node_index = jnp.arange(NODES_DEV, dtype=jnp.int32)
    slot_index = node_index // SLOT_NODES
    targets = block_target[:, :, slot_index]
    column = targets * COL_NODES + brick_y * NODES_DEV + brick_x * SLOT_NODES + (node_index % SLOT_NODES)[None, None, :]
    column = column.reshape(-1).astype(jnp.int32)
    trace_matrix = jnp.zeros((COMP, NODES), jnp.bfloat16).at[:, column].set(traces)
    trace_wide = trace_matrix.astype(jnp.float32)

    def block_rows(index):
        start = (index * SLAB_DEV).astype(jnp.int32)
        part_rows = lax.dynamic_slice_in_dim(boundary_matrix, start, SLAB_DEV, 1).astype(jnp.float32)
        products = jnp.dot(part_rows.reshape(2 * SLAB_DEV, NODES), trace_wide.T, preferred_element_type=jnp.float32)
        real_part = products[:SLAB_DEV]
        imag_part = products[SLAB_DEV:]
        return jnp.concatenate([real_part[:, :ANGLES] - imag_part[:, ANGLES:], imag_part[:, :ANGLES] + real_part[:, ANGLES:]], axis=1)

    blocks = lax.map(block_rows, jnp.arange(ROW_BLOCKS, dtype=jnp.int32))
    boundary_image = blocks.reshape(SLAB_ROWS, COMP)
    return volume_image, boundary_image
```

```python
import functools

import jax
import jax.numpy as jnp
from jax import lax
from jax.experimental import pallas as pl
from jax.experimental.pallas import tpu as pltpu
from jax.sharding import PartitionSpec as P

MESH = pl.DeviceIdType.MESH
F32 = jnp.float32
BF16 = jnp.bfloat16
GROUPS = 4


def iota(shape, dim):
    return lax.broadcasted_iota(jnp.int32, shape, dim)


def nt_dot(a, b):
    return lax.dot_general(a, b, (((1,), (1,)), ((), ())), preferred_element_type=F32)


def nn_dot(a, b):
    return lax.dot_general(a, b, (((1,), (0,)), ((), ())), preferred_element_type=F32)


def row_at(me_r, step, rows):
    wide = rows // 2
    if wide == 4:
        third = step % 3
        near = step < 6
        dz = jnp.where(near, step // 3, step - 6)
        dx = jnp.where(near, third + third // 2, 2)
    else:
        dz, dx = step // wide, step % wide
    z = (me_r // wide + dz) % 2
    x = (me_r % wide + dx) % wide
    return z * wide + x


def kernel(
    rows, cols,
    wave_in, medium_in, flux_in, cell_in, target_in, matrix_in,
    volume_out, boundary_out,
    wave, medium, flux, cell, target, matrix, onehot, picked, slots, traces, total, parts, landed,
    volume, faces, edges, corners, faces_in, edges_in, corners_in, faces_f, edges_f, corners_f,
    in_sem, out_sem, slot_send, slot_recv, row_send, row_recv, part_send, part_recv, halo_send, halo_recv,
):
    me_r = lax.axis_index("row")
    me_c = lax.axis_index("col")
    comps = wave.shape[0] // 32
    nodes = cell.shape[1]
    slot_len = nodes // cols
    half_slot = slot_len // 2
    span = cols // GROUPS
    my_group = me_c // span

    loads = [
        pltpu.make_async_copy(src, dst, in_sem.at[i])
        for i, (src, dst) in enumerate(
            [
                (cell_in, cell),
                (target_in, target),
                (wave_in, wave),
                (flux_in, flux),
                (medium_in, medium),
                (matrix_in, matrix),
            ]
        )
    ]
    for load in loads:
        load.start()

    barrier = pltpu.get_barrier_semaphore()

    def greet(r, c):
        pl.semaphore_signal(barrier, inc=1, device_id=(r, c), device_id_type=MESH)

    @pl.loop(1, cols)
    def _(i):
        greet(me_r, (me_c + i) % cols)

    @pl.loop(1, rows)
    def _(i):
        greet((me_r + i) % rows, me_c)

    partners = [(0, -1), (0, 1), (-1, 0), (1, 0), (-1, -1), (1, -1), (-1, 1), (1, 1)]

    def inside(step):
        dr, dc = step
        ok = None
        for d, me, n in ((dr, me_r, rows), (dc, me_c, cols)):
            if d:
                one = me + d >= 0 if d < 0 else me + d < n
                ok = one if ok is None else jnp.logical_and(ok, one)
        return ok

    for step in partners[4:]:

        @pl.when(inside(step))
        def _():
            greet(me_r + step[0], me_c + step[1])

    loads[0].wait()
    loads[1].wait()
    cells = cell[...]
    place = cells // 128
    onehot[...] = jnp.where(iota((128, nodes), 0) == cells % 128, 1.0, 0.0).astype(BF16)
    node = iota((1, nodes), 1)
    spread = jnp.where(iota((cols, nodes), 0) == iota((cols, nodes), 1) // slot_len, 1.0, 0.0)
    wanted = jnp.broadcast_to(target[...].astype(F32), (8, cols))
    wanted = nn_dot(wanted.astype(BF16), spread.astype(BF16))[:1].astype(jnp.int32)
    within = node % slot_len
    row_of = wanted * 8 + within % half_slot
    lane_half = within // half_slot

    loads[2].wait()
    here = iota((32, nodes), 0) == place

    @pl.loop(0, comps // 8)
    def _(i):
        start = pl.multiple_of(i * 256, 256)
        found = nn_dot(wave[pl.ds(start, 256), :].astype(BF16), onehot[...])
        found = jnp.where(here[None], found.reshape(8, 32, nodes), 0.0)
        found = found.reshape(8, 4, 8, nodes)
        found = (found[:, 0] + found[:, 1]) + (found[:, 2] + found[:, 3])
        picked[pl.ds(pl.multiple_of(i * 64, 64), 64), :] = found.reshape(64, nodes).astype(BF16)

    gather = jnp.where(iota((comps, comps * 8), 0) == iota((comps, comps * 8), 1) // 8, 1.0, 0.0)
    trace = nn_dot(gather.astype(BF16), picked[...])
    blank = jnp.zeros_like(trace)
    sent = None
    for half in range(2):
        match = jnp.logical_and(iota((cols * 8, nodes), 0) == row_of, lane_half == half)
        order = jnp.where(match, 1.0, 0.0).astype(BF16)
        pair = [trace, blank] if half == 0 else [blank, trace]
        term = nt_dot(order, jnp.concatenate(pair, axis=0).astype(BF16))
        sent = term if sent is None else sent + term
    slots[...] = sent.reshape(cols, 8, 2 * comps).astype(BF16)

    beside_r = jnp.where(me_r > 0, 1, 0) + jnp.where(me_r < rows - 1, 1, 0)
    beside_c = jnp.where(me_c > 0, 1, 0) + jnp.where(me_c < cols - 1, 1, 0)
    pl.semaphore_wait(barrier, cols - 1 + rows - 1 + beside_r * beside_c)

    def slot_copy(t):
        return pltpu.make_async_remote_copy(
            src_ref=slots.at[t],
            dst_ref=traces.at[me_r, me_c],
            send_sem=slot_send.at[t],
            recv_sem=slot_recv.at[me_c],
            device_id=(me_r, t),
            device_id_type=MESH,
        )

    def slot_arrival(c):
        return pltpu.make_async_remote_copy(
            src_ref=slots.at[c],
            dst_ref=traces.at[me_r, c],
            send_sem=slot_send.at[c],
            recv_sem=slot_recv.at[c],
            device_id=(me_r, c),
            device_id_type=MESH,
        )

    own_slot = pltpu.make_async_copy(slots.at[me_c], traces.at[me_r, me_c], slot_recv.at[me_c])
    for hop in (2, 1, 3, 0):
        first = ((my_group + hop) % GROUPS) * span

        @pl.loop(0, span)
        def _(i):
            t = first + i

            @pl.when(t != me_c)
            def _():
                slot_copy(t).start()

    own_slot.start()

    for side in range(2):

        @pl.loop(0, comps // 8)
        def _(i):
            rows_of = [wave[pl.ds(i * 256 + j * 32 + side * 24, 8), :] for j in range(8)]
            outer = jnp.concatenate(rows_of, axis=0).astype(BF16)
            faces[side, pl.ds(pl.multiple_of(i * 64, 64), 64), :] = outer

    for side in range(2):
        lane_y = 0 if side == 0 else 7
        edges[side] = wave[pl.ds(lane_y, comps * 4, stride=8), :].astype(BF16)
        corners[side] = wave[pl.ds(lane_y, comps, stride=32), :].astype(BF16)
        corners[2 + side] = wave[pl.ds(24 + lane_y, comps, stride=32), :].astype(BF16)

    halo_parts = [
        (faces.at[0], faces_in.at[1]),
        (faces.at[1], faces_in.at[0]),
        (edges.at[0], edges_in.at[1]),
        (edges.at[1], edges_in.at[0]),
        (corners.at[0], corners_in.at[3]),
        (corners.at[1], corners_in.at[2]),
        (corners.at[2], corners_in.at[1]),
        (corners.at[3], corners_in.at[0]),
    ]
    opposite = [1, 0, 3, 2, 7, 6, 5, 4]

    def halo_copy(k):
        return pltpu.make_async_remote_copy(
            src_ref=halo_parts[k][0],
            dst_ref=halo_parts[k][1],
            send_sem=halo_send.at[k],
            recv_sem=halo_recv.at[k],
            device_id=(me_r + partners[k][0], me_c + partners[k][1]),
            device_id_type=MESH,
        )

    for k in range(8):

        @pl.when(inside(partners[k]))
        def _():
            halo_copy(k).start()

    loads[3].wait()

    @pl.loop(0, comps // 8)
    def _(i):
        start = pl.multiple_of(i * 256, 256)
        wide = jnp.where(here[None], flux[pl.ds(i * 8, 8), :, :], 0.0).reshape(256, nodes)
        upper = wide.astype(BF16)
        lower = (wide - upper.astype(F32)).astype(BF16)
        volume[pl.ds(start, 256), :] = nt_dot(upper, onehot[...]) + nt_dot(lower, onehot[...])

    def row_copy(r, g):
        block = traces.at[me_r, pl.ds(g * span, span)]
        return pltpu.make_async_remote_copy(
            src_ref=block,
            dst_ref=block,
            send_sem=row_send.at[r, g],
            recv_sem=row_recv.at[me_r, g],
            device_id=(r, me_c),
            device_id_type=MESH,
        )

    def row_arrival(r, g):
        block = traces.at[r, pl.ds(g * span, span)]
        return pltpu.make_async_remote_copy(
            src_ref=block,
            dst_ref=block,
            send_sem=row_send.at[r, g],
            recv_sem=row_recv.at[r, g],
            device_id=(r, me_c),
            device_id_type=MESH,
        )

    for hop in (0, 1, 3, 2):
        g = (my_group + hop) % GROUPS

        @pl.loop(0, span)
        def _(i):
            slot_arrival(g * span + i).wait_recv()

        @pl.loop(1, rows)
        def _(i):
            row_copy(row_at(me_r, rows - i, rows), g).start()

    loads[5].wait()
    total[...] = jnp.zeros_like(total)
    left = iota((cols * 8, 128), 1) < comps
    minus = iota((cols * 8, 128), 1) % comps < comps // 2
    to_node = iota((nodes, cols * 8), 0)
    packed = iota((nodes, cols * 8), 1)
    unpack = []
    for half in range(2):
        hit = jnp.logical_and(
            to_node == (packed // 8) * slot_len + packed % 8 + half * half_slot,
            packed % 8 < half_slot,
        )
        unpack.append(jnp.where(hit, 1.0, 0.0).astype(BF16))
    unpack = jnp.concatenate(unpack, axis=1)

    @pl.loop(0, rows)
    def _(step):
        r = row_at(me_r, step, rows)

        @pl.when(step > 0)
        def _():
            @pl.loop(0, GROUPS)
            def _(g):
                row_arrival(r, g).wait_recv()

        raw = traces[r].reshape(cols * 8, 2 * comps).astype(F32)
        turned = pltpu.roll(raw, comps, 1)
        stacked = []
        for half in range(2):
            same = jnp.where(left, raw, turned) if half == 0 else jnp.where(left, turned, raw)
            swapped = pltpu.roll(same, comps // 2, 1)
            swapped = jnp.where(minus, -swapped, swapped)
            stacked.append(jnp.concatenate([same, swapped], axis=1).astype(BF16))
        both = nn_dot(unpack, jnp.concatenate(stacked, axis=0)).astype(BF16)
        columns = pl.ds(pl.multiple_of(r * nodes, nodes), nodes)
        total[...] += nn_dot(matrix[0, :, columns], both[:, :128]) + nn_dot(
            matrix[1, :, columns], both[:, 128:]
        )

    tiles = total[...].reshape(cols, 2, 8, 128)
    parts[...] = jnp.where(
        iota((cols, 8, 128), 2) < comps, tiles[:, 0], tiles[:, 1]
    ).astype(BF16)

    def part_copy(t):
        return pltpu.make_async_remote_copy(
            src_ref=parts.at[t],
            dst_ref=landed.at[me_c],
            send_sem=part_send.at[t],
            recv_sem=part_recv.at[me_c],
            device_id=(me_r, t),
            device_id_type=MESH,
        )

    def part_arrival(c):
        return pltpu.make_async_remote_copy(
            src_ref=parts.at[c],
            dst_ref=landed.at[c],
            send_sem=part_send.at[c],
            recv_sem=part_recv.at[c],
            device_id=(me_r, c),
            device_id_type=MESH,
        )

    own_part = pltpu.make_async_copy(parts.at[me_c], landed.at[me_c], part_recv.at[me_c])
    for hop in (2, 1, 3, 0):
        first = ((my_group + hop) % GROUPS) * span

        @pl.loop(0, span)
        def _(i):
            t = first + i

            @pl.when(t != me_c)
            def _():
                part_copy(t).start()

    own_part.start()

    spread_to = [faces_f.at[0], faces_f.at[1], edges_f.at[0], edges_f.at[1]] + [
        corners_f.at[k] for k in range(4)
    ]
    come_from = [faces_in.at[0], faces_in.at[1], edges_in.at[0], edges_in.at[1]] + [
        corners_in.at[k] for k in range(4)
    ]
    for k in range(8):

        @pl.when(inside(partners[k]))
        def _():
            halo = pltpu.make_async_remote_copy(
                src_ref=come_from[k],
                dst_ref=come_from[k],
                send_sem=halo_send.at[k],
                recv_sem=halo_recv.at[opposite[k]],
                device_id=(me_r + partners[k][0], me_c + partners[k][1]),
                device_id_type=MESH,
            )
            halo.wait_recv()
            spread_to[k][...] = come_from[k][...].astype(F32)

        @pl.when(jnp.logical_not(inside(partners[k])))
        def _():
            spread_to[k][...] = jnp.zeros(spread_to[k].shape, F32)

    loads[4].wait()
    sublane = iota((8, 128), 0)
    lane = iota((8, 128), 1)

    def depth_sides(v):
        below = jnp.where(lane == 0, 0.0, pltpu.roll(v, 1, 1))
        above = jnp.where(lane == 127, 0.0, pltpu.roll(v, 127, 1))
        return below + above

    def layer(u, low, high):
        below = jnp.where(sublane == 0, jnp.broadcast_to(low, (8, 128)), pltpu.roll(u, 1, 0))
        above = jnp.where(sublane == 7, jnp.broadcast_to(high, (8, 128)), pltpu.roll(u, 7, 0))
        sides = below + above
        outer = depth_sides(sides)
        ring = 2.0 * (sides + depth_sides(u)) + outer
        return u, outer, ring, 4.0 * u + ring

    @pl.loop(0, comps)
    def _(k):
        layers = []
        for x in range(6):
            if x in (0, 5):
                side = 0 if x == 0 else 1
                u = faces_f[side, pl.ds(pl.multiple_of(k * 8, 8), 8), :]
                low = corners_f[2 * side, pl.ds(k, 1), :]
                high = corners_f[2 * side + 1, pl.ds(k, 1), :]
            else:
                u = wave[pl.ds(pl.multiple_of(k * 32 + (x - 1) * 8, 8), 8), :]
                low = edges_f[0, pl.ds(k * 4 + x - 1, 1), :]
                high = edges_f[1, pl.ds(k * 4 + x - 1, 1), :]
            layers.append(layer(u, low, high))
        for x in range(1, 5):
            u, outer, ring, mass = layers[x]
            stiffness = (8.0 / 3.0) * u - (1.0 / 6.0) * outer
            stiffness -= (1.0 / 12.0) * (layers[x - 1][2] + layers[x + 1][2])
            mass_sum = (2.0 * mass + (layers[x - 1][3] + layers[x + 1][3])) * (1.0 / 27.0)
            where = pl.ds(pl.multiple_of(k * 32 + (x - 1) * 8, 8), 8)
            volume[where, :] = (
                stiffness - medium[pl.ds((x - 1) * 8, 8), :] * mass_sum - volume[where, :]
            )

    store = pltpu.make_async_copy(volume, volume_out, out_sem)
    store.start()

    @pl.loop(0, cols)
    def _(c):
        part_arrival(c).wait_recv()

    sums = jnp.sum(landed[...].astype(F32), axis=0)
    boundary_out[0:8, :] = sums[:, :comps]
    boundary_out[8:16, :] = pltpu.roll(sums, comps, 1)[:, :comps]

    @pl.loop(0, cols)
    def _(t):
        @pl.when(t != me_c)
        def _():
            slot_copy(t).wait_send()
            part_copy(t).wait_send()

    @pl.loop(1, rows)
    def _(i):
        @pl.loop(0, GROUPS)
        def _(g):
            row_copy((me_r + i) % rows, g).wait_send()

    for k in range(8):

        @pl.when(inside(partners[k]))
        def _():
            halo_copy(k).wait_send()

    store.wait()


def on_device(rows, cols, wave_field, medium_term, node_flux, node_cell, block_target, boundary_matrix):
    comps = wave_field.shape[0]
    nodes = node_cell.shape[-1]
    slab_rows, width = boundary_matrix.shape[1:]
    own_rows = slab_rows // cols
    vmem = pltpu.VMEM
    dma = pltpu.SemaphoreType.DMA
    volume, boundary = pl.pallas_call(
        functools.partial(kernel, rows, cols),
        out_shape=(
            jax.ShapeDtypeStruct((comps * 32, 128), F32),
            jax.ShapeDtypeStruct((own_rows, comps), F32),
        ),
        in_specs=[pl.BlockSpec(memory_space=pltpu.HBM)] * 6,
        out_specs=(pl.BlockSpec(memory_space=pltpu.HBM), pl.BlockSpec(memory_space=pltpu.VMEM)),
        scratch_shapes=[
            vmem((comps * 32, 128), F32),
            vmem((32, 128), F32),
            vmem((comps, 1, nodes), F32),
            vmem((1, nodes), jnp.int32),
            vmem((1, cols), jnp.int32),
            vmem((2, slab_rows, width), BF16),
            vmem((128, nodes), BF16),
            vmem((comps * 8, nodes), BF16),
            vmem((cols, 8, 128), BF16),
            vmem((rows, cols, 8, 128), BF16),
            vmem((slab_rows, 128), F32),
            vmem((cols, 8, 128), BF16),
            vmem((cols, 8, 128), BF16),
            vmem((comps * 32, 128), F32),
            vmem((2, comps * 8, 128), BF16),
            vmem((2, comps * 4, 128), BF16),
            vmem((4, comps, 128), BF16),
            vmem((2, comps * 8, 128), BF16),
            vmem((2, comps * 4, 128), BF16),
            vmem((4, comps, 128), BF16),
            vmem((2, comps * 8, 128), F32),
            vmem((2, comps * 4, 128), F32),
            vmem((4, comps, 128), F32),
            dma((6,)),
            dma(()),
            dma((cols,)),
            dma((cols,)),
            dma((rows, GROUPS)),
            dma((rows, GROUPS)),
            dma((cols,)),
            dma((cols,)),
            dma((8,)),
            dma((8,)),
        ],
        compiler_params=pltpu.CompilerParams(
            collective_id=0, has_side_effects=True, vmem_limit_bytes=63_000_000
        ),
        name="coupled_apply",
    )(
        wave_field.reshape(comps * 32, 128),
        medium_term.reshape(32, 128),
        node_flux.reshape(comps, 1, nodes),
        node_cell.reshape(1, nodes),
        block_target.reshape(1, cols),
        boundary_matrix,
    )
    return volume.reshape(wave_field.shape), boundary


def solution(mesh):
    in_specs = (
        P(None, "col", "row", None),
        P("col", "row", None),
        P(None, "col", "row", None),
        P("col", "row", None),
        P("col", "row", None),
        P(None, "row", "col"),
    )
    out_specs = (P(None, "col", "row", None), P(("row", "col"), None))
    return jax.shard_map(
        functools.partial(on_device, mesh.shape["row"], mesh.shape["col"]),
        mesh=mesh,
        in_specs=in_specs,
        out_specs=out_specs,
        check_vma=False,
    )
```

```python
import functools

import jax
import jax.numpy as jnp
from jax import lax
from jax.experimental import pallas as pl
from jax.experimental.pallas import tpu as pltpu
from jax.sharding import PartitionSpec as P

MESH = pl.DeviceIdType.MESH
F32 = jnp.float32
BF16 = jnp.bfloat16
GROUPS = 4


def iota(shape, dim):
    return lax.broadcasted_iota(jnp.int32, shape, dim)


def nt_dot(a, b):
    return lax.dot_general(a, b, (((1,), (1,)), ((), ())), preferred_element_type=F32)


def nn_dot(a, b):
    return lax.dot_general(a, b, (((1,), (0,)), ((), ())), preferred_element_type=F32)


def row_at(me_r, step, rows):
    wide = rows // 2
    if wide == 4:
        third = step % 3
        near = step < 6
        dz = jnp.where(near, step // 3, step - 6)
        dx = jnp.where(near, third + third // 2, 2)
    else:
        dz, dx = step // wide, step % wide
    z = (me_r // wide + dz) % 2
    x = (me_r % wide + dx) % wide
    return z * wide + x


def kernel(
    rows, cols,
    wave_in, medium_in, flux_in, cell_in, target_in, matrix_in,
    volume, boundary_out,
    wave, medium, flux, cell, target, matrix, onehot, picked, unpack, slots, near, relay, traces,
    total, parts, landed,
    faces, edges, faces_in, edges_in, corners_in, faces_f, edges_f, corners_f,
    in_sem, near_send, near_recv, pass_send, pass_recv, own_sem, row_send, row_recv, part_send, part_recv,
    halo_send, halo_recv,
):
    me_r = lax.axis_index("row")
    me_c = lax.axis_index("col")
    comps = wave.shape[0] // 32
    nodes = cell.shape[1]
    slot_len = nodes // cols
    half_slot = slot_len // 2
    span = cols // GROUPS
    mine = me_c // span
    me_n = me_c % span
    after, across, before = [(mine + d) % GROUPS for d in (1, 2, 3)]

    loads = [
        pltpu.make_async_copy(src, dst, in_sem.at[i])
        for i, (src, dst) in enumerate(
            [
                (cell_in, cell),
                (target_in, target),
                (wave_in, wave),
                (flux_in, flux),
                (medium_in, medium),
                (matrix_in, matrix),
            ]
        )
    ]
    for load in loads:
        load.start()

    barrier = pltpu.get_barrier_semaphore()

    def greet(r, c):
        pl.semaphore_signal(barrier, inc=1, device_id=(r, c), device_id_type=MESH)

    greet(me_r, after * span + me_n)
    greet(me_r, before * span + me_n)

    @pl.loop(1, rows)
    def _(i):
        greet((me_r + i) % rows, me_c)

    @pl.loop(1, span)
    def _(i):
        greet(me_r, mine * span + (me_n + i) % span)

    def remote(src, dst, send_sem, recv_sem, r, c):
        return pltpu.make_async_remote_copy(
            src_ref=src,
            dst_ref=dst,
            send_sem=send_sem,
            recv_sem=recv_sem,
            device_id=(r, c),
            device_id_type=MESH,
        )

    loads[0].wait()
    loads[1].wait()
    cells = cell[...]
    place = cells // 128
    onehot[...] = jnp.where(iota((128, nodes), 0) == cells % 128, 1.0, 0.0).astype(BF16)
    node = iota((1, nodes), 1)
    spread = jnp.where(iota((cols, nodes), 0) == iota((cols, nodes), 1) // slot_len, 1.0, 0.0)
    wanted = jnp.broadcast_to(target[...].astype(F32), (8, cols))
    wanted = nn_dot(wanted.astype(BF16), spread.astype(BF16))[:1].astype(jnp.int32)
    within = node % slot_len
    row_of = ((wanted % span) * GROUPS + wanted // span) * 8 + within % half_slot
    lane_half = within // half_slot

    loads[2].wait()
    here = iota((32, nodes), 0) == place

    @pl.loop(0, comps // 8)
    def _(i):
        start = pl.multiple_of(i * 256, 256)
        found = nn_dot(wave[pl.ds(start, 256), :].astype(BF16), onehot[...])
        found = jnp.where(here[None], found.reshape(8, 32, nodes), 0.0)
        found = found.reshape(8, 4, 8, nodes)
        found = (found[:, 0] + found[:, 1]) + (found[:, 2] + found[:, 3])
        picked[pl.ds(pl.multiple_of(i * 64, 64), 64), :] = found.reshape(64, nodes).astype(BF16)

    gather = jnp.where(iota((comps, comps * 8), 0) == iota((comps, comps * 8), 1) // 8, 1.0, 0.0)
    trace = nn_dot(gather.astype(BF16), picked[...])
    blank = jnp.zeros_like(trace)
    sent = None
    for half in range(2):
        match = jnp.logical_and(iota((cols * 8, nodes), 0) == row_of, lane_half == half)
        order = jnp.where(match, 1.0, 0.0).astype(BF16)
        pair = [trace, blank] if half == 0 else [blank, trace]
        term = nt_dot(order, jnp.concatenate(pair, axis=0).astype(BF16))
        sent = term if sent is None else sent + term
    slots[...] = sent.reshape(span, GROUPS, 8, 2 * comps).astype(BF16)

    pl.semaphore_wait(barrier, span - 1 + 2 + rows - 1)

    def near_copy(n, source):
        return remote(
            slots.at[n], near.at[:, source], near_send.at[n], near_recv.at[source], me_r, mine * span + n
        )

    @pl.loop(1, span)
    def _(i):
        near_copy((me_n + span - i) % span, me_n).start()

    own_slots = pltpu.make_async_copy(slots.at[me_n], near.at[:, me_n], near_recv.at[me_n])
    own_slots.start()

    has = [me_c > 0, me_c < cols - 1, me_r > 0, me_r < rows - 1]
    for side in range(2):
        for x in range(4):
            edges[side, x] = wave[pl.ds(x * 8 + side * 7, comps, stride=32), :].astype(BF16)

    def edge_copy(side):
        return remote(
            edges.at[side],
            edges_in.at[1 - side],
            halo_send.at[2 + side],
            halo_recv.at[2 + side],
            me_r + 2 * side - 1,
            me_c,
        )

    for side in range(2):

        @pl.when(has[2 + side])
        def _():
            edge_copy(side).start()

    for side in range(2):

        @pl.loop(0, comps // 8)
        def _(i):
            rows_of = [wave[pl.ds(i * 256 + j * 32 + side * 24, 8), :] for j in range(8)]
            outer = jnp.concatenate(rows_of, axis=0).astype(BF16)
            faces[side, pl.ds(pl.multiple_of(i * 64, 64), 64), :] = outer

    @pl.loop(0, span)
    def _(i):
        near_copy(i, i).wait_recv()

    cut = span // 2

    def whole(g):
        return pl.ds(g * span, span)

    def pass_on(k):
        first, second = (pl.ds(0, cut), pl.ds(cut, span - cut))
        source, target_at, group = [
            (near.at[across, first], relay.at[first], after),
            (near.at[across, second], relay.at[second], before),
            (near.at[after], traces.at[me_r, whole(mine)], after),
            (near.at[before], traces.at[me_r, whole(mine)], before),
            (relay.at[first], traces.at[me_r, pl.ds(before * span, cut)], after),
            (relay.at[second], traces.at[me_r, pl.ds(after * span + cut, span - cut)], before),
        ][k]
        return remote(
            source, target_at, pass_send.at[k], pass_recv.at[k], me_r, group * span + me_n
        )

    def passed(k):
        first, second = (pl.ds(0, cut), pl.ds(cut, span - cut))
        ref, group = [
            (relay.at[first], before),
            (relay.at[second], after),
            (traces.at[me_r, whole(before)], before),
            (traces.at[me_r, whole(after)], after),
            (traces.at[me_r, pl.ds(across * span, cut)], before),
            (traces.at[me_r, pl.ds(across * span + cut, span - cut)], after),
        ][k]
        return remote(ref, ref, pass_send.at[k], pass_recv.at[k], me_r, group * span + me_n)

    halves = [k for k in (0, 1) if k == 1 or cut > 0]
    for k in halves:
        pass_on(k).start()
    pass_on(2).start()
    pass_on(3).start()
    own_group = pltpu.make_async_copy(near.at[mine], traces.at[me_r, whole(mine)], own_sem)
    own_group.start()

    def row_copy(r, g, source):
        return remote(
            source, traces.at[me_r, whole(g)], row_send.at[r, g], row_recv.at[me_r, g], r, me_c
        )

    def row_arrival(r, g):
        ref = traces.at[r, whole(g)]
        return remote(ref, ref, row_send.at[r, g], row_recv.at[r, g], r, me_c)

    def to_rows(g, source):
        @pl.loop(1, rows)
        def _(i):
            row_copy(row_at(me_r, rows - i, rows), g, source).start()

    to_rows(mine, near.at[mine])

    loads[3].wait()

    @pl.loop(0, comps // 8)
    def _(i):
        start = pl.multiple_of(i * 256, 256)
        wide = jnp.where(here[None], flux[pl.ds(i * 8, 8), :, :], 0.0).reshape(256, nodes)
        upper = wide.astype(BF16)
        lower = (wide - upper.astype(F32)).astype(BF16)
        volume[pl.ds(start, 256), :] = nt_dot(upper, onehot[...]) + nt_dot(lower, onehot[...])

    for k in halves:
        passed(k).wait_recv()
        pass_on(4 + k).start()

    def face_copy(side):
        return remote(
            faces.at[side],
            faces_in.at[1 - side],
            halo_send.at[side],
            halo_recv.at[side],
            me_r,
            me_c + 2 * side - 1,
        )

    for side in range(2):

        @pl.when(has[side])
        def _():
            face_copy(side).start()

    for k, g in ((2, before), (3, after)):
        passed(k).wait_recv()
        to_rows(g, traces.at[me_r, whole(g)])

    packed_rows = cols // 2 * 8
    window, shift = nodes * 2 // 3, nodes // 6
    at_row = iota((window, packed_rows), 0)
    packed = iota((window, packed_rows), 1)
    for part in range(2):
        for half in range(2):
            hit = jnp.logical_and(
                at_row - part * shift == (packed // 8) * slot_len + packed % 8 + half * half_slot,
                packed % 8 < half_slot,
            )
            unpack[part, :, half * packed_rows : (half + 1) * packed_rows] = jnp.where(
                hit, 1.0, 0.0
            ).astype(BF16)
    total[...] = jnp.zeros_like(total)

    for k in halves:
        passed(4 + k).wait_recv()
    to_rows(across, traces.at[me_r, whole(across)])

    def corner_copy(side, way):
        return remote(
            edges_in.at[side, 3 * way],
            corners_in.at[2 - 2 * way + side],
            halo_send.at[4 + 2 * side + way],
            halo_recv.at[4 + 2 * side + way],
            me_r,
            me_c + 2 * way - 1,
        )

    for side in range(2):

        @pl.when(has[2 + side])
        def _():
            ref = edges_in.at[side]
            remote(
                ref, ref, halo_send.at[3 - side], halo_recv.at[3 - side], me_r + 2 * side - 1, me_c
            ).wait_recv()
            for way in range(2):

                @pl.when(has[way])
                def _():
                    corner_copy(side, way).start()

    own_group.wait()
    loads[5].wait()
    left = iota((packed_rows, 128), 1) < comps
    minus = iota((packed_rows, 128), 1) % comps < comps // 2
    for late in range(2):
        part = (mine // 2 + late) % 2

        @pl.loop(0, rows)
        def _(step):
            r = row_at(me_r, step, rows)

            @pl.when(step > 0)
            def _():
                row_arrival(r, 2 * part).wait_recv()
                row_arrival(r, 2 * part + 1).wait_recv()

            raw = traces[r, pl.ds(part * (cols // 2), cols // 2)]
            raw = raw.reshape(packed_rows, 2 * comps).astype(F32)
            turned = pltpu.roll(raw, comps, 1)
            stacked = []
            for half in range(2):
                same = jnp.where(left, raw, turned) if half == 0 else jnp.where(left, turned, raw)
                swapped = pltpu.roll(same, comps // 2, 1)
                swapped = jnp.where(minus, -swapped, swapped)
                stacked.append(jnp.concatenate([same, swapped], axis=1).astype(BF16))
            both = nn_dot(unpack[part], jnp.concatenate(stacked, axis=0)).astype(BF16)
            columns = pl.ds(pl.multiple_of(r * nodes + part * (nodes // 3), nodes // 3), window)
            total[...] += nn_dot(matrix[0, :, columns], both[:, :128]) + nn_dot(
                matrix[1, :, columns], both[:, 128:]
            )

    tiles = total[...].reshape(cols, 2, 8, 128)
    parts[...] = jnp.where(
        iota((cols, 8, 128), 2) < comps, tiles[:, 0], tiles[:, 1]
    ).astype(BF16)

    def part_copy(t, source):
        return remote(
            parts.at[t], landed.at[source], part_send.at[t], part_recv.at[source], me_r, t
        )

    for hop in (2, 1, 3, 0):
        first = ((mine + hop) % GROUPS) * span

        @pl.loop(0, span)
        def _(i):
            t = first + i

            @pl.when(t != me_c)
            def _():
                part_copy(t, me_c).start()

    own_part = pltpu.make_async_copy(parts.at[me_c], landed.at[me_c], part_recv.at[me_c])
    own_part.start()

    halos = [
        (faces_in.at[1 - side], faces_f.at[1 - side], side, has[1 - side], (0, 1 - 2 * side))
        for side in range(2)
    ]
    halos += [
        (edges_in.at[side], edges_f.at[side], -1, has[2 + side], None) for side in range(2)
    ]
    halos += [
        (
            corners_in.at[2 - 2 * way + side],
            corners_f.at[2 - 2 * way + side],
            4 + 2 * side + way,
            jnp.logical_and(has[1 - way], has[2 + side]),
            (0, 1 - 2 * way),
        )
        for side in range(2)
        for way in range(2)
    ]
    for got, kept, k, there, step in halos:

        @pl.when(there)
        def _():
            if step is not None:
                remote(
                    got, got, halo_send.at[k], halo_recv.at[k], me_r + step[0], me_c + step[1]
                ).wait_recv()
            kept[...] = got[...].astype(F32)

        @pl.when(jnp.logical_not(there))
        def _():
            kept[...] = jnp.zeros(kept.shape, F32)

    loads[4].wait()
    sublane = iota((8, 128), 0)
    lane = iota((8, 128), 1)

    def depth_sides(v):
        below = jnp.where(lane == 0, 0.0, pltpu.roll(v, 1, 1))
        above = jnp.where(lane == 127, 0.0, pltpu.roll(v, 127, 1))
        return below + above

    def layer(u, low, high):
        below = jnp.where(sublane == 0, jnp.broadcast_to(low, (8, 128)), pltpu.roll(u, 1, 0))
        above = jnp.where(sublane == 7, jnp.broadcast_to(high, (8, 128)), pltpu.roll(u, 7, 0))
        sides = below + above
        outer = depth_sides(sides)
        ring = 2.0 * (sides + depth_sides(u)) + outer
        return u, outer, ring, 4.0 * u + ring

    @pl.loop(0, comps)
    def _(k):
        layers = []
        for x in range(6):
            if x in (0, 5):
                side = 0 if x == 0 else 1
                u = faces_f[side, pl.ds(pl.multiple_of(k * 8, 8), 8), :]
                low = corners_f[2 * side, pl.ds(k, 1), :]
                high = corners_f[2 * side + 1, pl.ds(k, 1), :]
            else:
                u = wave[pl.ds(pl.multiple_of(k * 32 + (x - 1) * 8, 8), 8), :]
                low = edges_f[0, x - 1, pl.ds(k, 1), :]
                high = edges_f[1, x - 1, pl.ds(k, 1), :]
            layers.append(layer(u, low, high))
        for x in range(1, 5):
            u, outer, ring, mass = layers[x]
            stiffness = (8.0 / 3.0) * u - (1.0 / 6.0) * outer
            stiffness -= (1.0 / 12.0) * (layers[x - 1][2] + layers[x + 1][2])
            mass_sum = (2.0 * mass + (layers[x - 1][3] + layers[x + 1][3])) * (1.0 / 27.0)
            where = pl.ds(pl.multiple_of(k * 32 + (x - 1) * 8, 8), 8)
            volume[where, :] = (
                stiffness - medium[pl.ds((x - 1) * 8, 8), :] * mass_sum - volume[where, :]
            )

    @pl.loop(1, span)
    def _(i):
        near_copy((me_n + i) % span, me_n).wait_send()

    for k in halves:
        pass_on(k).wait_send()
        pass_on(4 + k).wait_send()
    pass_on(2).wait_send()
    pass_on(3).wait_send()

    @pl.loop(1, rows)
    def _(i):
        @pl.loop(0, GROUPS)
        def _(g):
            row_copy((me_r + i) % rows, g, traces.at[me_r, whole(g)]).wait_send()

    for side in range(2):

        @pl.when(has[side])
        def _():
            face_copy(side).wait_send()

        @pl.when(has[2 + side])
        def _():
            edge_copy(side).wait_send()
            for way in range(2):

                @pl.when(has[way])
                def _():
                    corner_copy(side, way).wait_send()

    @pl.loop(0, cols)
    def _(c):
        part_copy(c, c).wait_recv()

    sums = jnp.sum(landed[...].astype(F32), axis=0)
    boundary_out[0:8, :] = sums[:, :comps]
    boundary_out[8:16, :] = pltpu.roll(sums, comps, 1)[:, :comps]

    @pl.loop(0, cols)
    def _(t):
        @pl.when(t != me_c)
        def _():
            part_copy(t, me_c).wait_send()


def on_device(rows, cols, wave_field, medium_term, node_flux, node_cell, block_target, boundary_matrix):
    comps = wave_field.shape[0]
    nodes = node_cell.shape[-1]
    slab_rows, width = boundary_matrix.shape[1:]
    own_rows = slab_rows // cols
    vmem = pltpu.VMEM
    dma = pltpu.SemaphoreType.DMA
    volume, boundary = pl.pallas_call(
        functools.partial(kernel, rows, cols),
        out_shape=(
            pltpu.VMEM((comps * 32, 128), F32),
            pltpu.VMEM((own_rows, comps), F32),
        ),
        in_specs=[pl.BlockSpec(memory_space=pltpu.HBM)] * 6,
        out_specs=(pl.BlockSpec(memory_space=pltpu.VMEM), pl.BlockSpec(memory_space=pltpu.VMEM)),
        scratch_shapes=[
            vmem((comps * 32, 128), F32),
            vmem((32, 128), F32),
            vmem((comps, 1, nodes), F32),
            vmem((1, nodes), jnp.int32),
            vmem((1, cols), jnp.int32),
            vmem((2, slab_rows, width), BF16),
            vmem((128, nodes), BF16),
            vmem((comps * 8, nodes), BF16),
            vmem((2, nodes * 2 // 3, cols * 8), BF16),
            vmem((cols // GROUPS, GROUPS, 8, 128), BF16),
            vmem((GROUPS, cols // GROUPS, 8, 128), BF16),
            vmem((cols // GROUPS, 8, 128), BF16),
            vmem((rows, cols, 8, 128), BF16),
            vmem((slab_rows, 128), F32),
            vmem((cols, 8, 128), BF16),
            vmem((cols, 8, 128), BF16),
            vmem((2, comps * 8, 128), BF16),
            vmem((2, 4, comps, 128), BF16),
            vmem((2, comps * 8, 128), BF16),
            vmem((2, 4, comps, 128), BF16),
            vmem((4, comps, 128), BF16),
            vmem((2, comps * 8, 128), F32),
            vmem((2, 4, comps, 128), F32),
            vmem((4, comps, 128), F32),
            dma((6,)),
            dma((cols // GROUPS,)),
            dma((cols // GROUPS,)),
            dma((6,)),
            dma((6,)),
            dma(()),
            dma((rows, GROUPS)),
            dma((rows, GROUPS)),
            dma((cols,)),
            dma((cols,)),
            dma((8,)),
            dma((8,)),
        ],
        compiler_params=pltpu.CompilerParams(
            collective_id=0, has_side_effects=True, vmem_limit_bytes=48 * 2**20
        ),
        name="coupled_apply",
    )(
        *[
            pltpu.with_memory_space_constraint(x, pltpu.HBM)
            for x in (
                wave_field.reshape(comps * 32, 128),
                medium_term.reshape(32, 128),
                node_flux.reshape(comps, 1, nodes),
                node_cell.reshape(1, nodes),
                block_target.reshape(1, cols),
                boundary_matrix,
            )
        ]
    )
    return volume.reshape(wave_field.shape), boundary


def solution(mesh):
    in_specs = (
        P(None, "col", "row", None),
        P("col", "row", None),
        P(None, "col", "row", None),
        P("col", "row", None),
        P("col", "row", None),
        P(None, "row", "col"),
    )
    out_specs = (P(None, "col", "row", None), P(("row", "col"), None))
    return jax.shard_map(
        functools.partial(on_device, mesh.shape["row"], mesh.shape["col"]),
        mesh=mesh,
        in_specs=in_specs,
        out_specs=out_specs,
        check_vma=False,
    )
```

```python
import functools

import jax
import jax.numpy as jnp
from jax import lax
from jax.experimental import pallas as pl
from jax.experimental.pallas import tpu as pltpu
from jax.sharding import PartitionSpec as P

MESH = pl.DeviceIdType.MESH
F32 = jnp.float32
BF16 = jnp.bfloat16
GROUPS = 4


def iota(shape, dim):
    return lax.broadcasted_iota(jnp.int32, shape, dim)


def nt_dot(a, b):
    return lax.dot_general(a, b, (((1,), (1,)), ((), ())), preferred_element_type=F32)


def nn_dot(a, b):
    return lax.dot_general(a, b, (((1,), (0,)), ((), ())), preferred_element_type=F32)


def kernel(
    rows, cols,
    wave_in, medium_in, flux_in, cell_in, target_in, matrix_in,
    volume, boundary_out,
    wave, medium, flux, cell, target, matrix, onehot, picked, unpack, placed, slots, near, relay, traces,
    total, parts, landed,
    faces, edges, faces_in, edges_in, corners_in, faces_f, edges_f, corners_f,
    in_sem, near_send, near_recv, pass_send, pass_recv, own_sem, row_send, row_recv, part_send, part_recv,
    halo_send, halo_recv,
):
    me_r = lax.axis_index("row")
    me_c = lax.axis_index("col")
    comps = wave.shape[0] // 32
    nodes = cell.shape[1]
    slot_len = nodes // cols
    half_slot = slot_len // 2
    span = cols // GROUPS
    mine = me_c // span
    me_n = me_c % span
    after, across, before = [(mine + d) % GROUPS for d in (1, 2, 3)]

    loads = [
        pltpu.make_async_copy(src, dst, in_sem.at[i])
        for i, (src, dst) in enumerate(
            [
                (cell_in, cell),
                (target_in, target),
                (wave_in, wave),
                (flux_in, flux),
                (medium_in, medium),
                (matrix_in, matrix),
            ]
        )
    ]
    for load in loads:
        load.start()

    barrier = pltpu.get_barrier_semaphore()

    def greet(r, c):
        pl.semaphore_signal(barrier, inc=1, device_id=(r, c), device_id_type=MESH)

    greet(me_r, after * span + me_n)
    greet(me_r, before * span + me_n)

    @pl.loop(1, rows)
    def _(i):
        greet((me_r + i) % rows, me_c)

    @pl.loop(1, span)
    def _(i):
        greet(me_r, mine * span + (me_n + i) % span)

    def remote(src, dst, send_sem, recv_sem, r, c):
        return pltpu.make_async_remote_copy(
            src_ref=src,
            dst_ref=dst,
            send_sem=send_sem,
            recv_sem=recv_sem,
            device_id=(r, c),
            device_id_type=MESH,
        )

    loads[0].wait()
    loads[1].wait()
    cells = cell[...]
    place = cells // 128
    onehot[...] = jnp.where(iota((128, nodes), 0) == cells % 128, 1.0, 0.0).astype(BF16)
    node = iota((1, nodes), 1)
    spread = jnp.where(iota((cols, nodes), 0) == iota((cols, nodes), 1) // slot_len, 1.0, 0.0)
    wanted = jnp.broadcast_to(target[...].astype(F32), (8, cols))
    wanted = nn_dot(wanted.astype(BF16), spread.astype(BF16))[:1].astype(jnp.int32)
    within = node % slot_len
    row_of = ((wanted % span) * GROUPS + wanted // span) * 8 + within % half_slot
    lane_half = within // half_slot

    loads[2].wait()
    here = iota((32, nodes), 0) == place

    @pl.loop(0, comps // 8)
    def _(i):
        start = pl.multiple_of(i * 256, 256)
        found = nn_dot(wave[pl.ds(start, 256), :].astype(BF16), onehot[...])
        found = jnp.where(here[None], found.reshape(8, 32, nodes), 0.0)
        found = found.reshape(8, 4, 8, nodes)
        found = (found[:, 0] + found[:, 1]) + (found[:, 2] + found[:, 3])
        picked[pl.ds(pl.multiple_of(i * 64, 64), 64), :] = found.reshape(64, nodes).astype(BF16)

    gather = jnp.where(iota((comps, comps * 8), 0) == iota((comps, comps * 8), 1) // 8, 1.0, 0.0)
    trace = nn_dot(gather.astype(BF16), picked[...])
    blank = jnp.zeros_like(trace)
    sent = None
    for half in range(2):
        match = jnp.logical_and(iota((cols * 8, nodes), 0) == row_of, lane_half == half)
        order = jnp.where(match, 1.0, 0.0).astype(BF16)
        pair = [trace, blank] if half == 0 else [blank, trace]
        term = nt_dot(order, jnp.concatenate(pair, axis=0).astype(BF16))
        sent = term if sent is None else sent + term
    slots[...] = sent.reshape(span, GROUPS, 8, 2 * comps).astype(BF16)

    pl.semaphore_wait(barrier, span - 1 + 2 + rows - 1)

    def near_copy(n, source):
        return remote(
            slots.at[n], near.at[:, source], near_send, near_recv, me_r, mine * span + n
        )

    @pl.loop(1, span)
    def _(i):
        near_copy((me_n + span - i) % span, me_n).start()

    own_slots = pltpu.make_async_copy(slots.at[me_n], near.at[:, me_n], near_recv)
    own_slots.start()

    has = [me_c > 0, me_c < cols - 1, me_r > 0, me_r < rows - 1]
    for side in range(2):
        for x in range(4):
            edges[side, x] = wave[pl.ds(x * 8 + side * 7, comps, stride=32), :].astype(BF16)

    def edge_copy(side):
        return remote(
            edges.at[side],
            edges_in.at[1 - side],
            halo_send.at[2 + side],
            halo_recv.at[2 + side],
            me_r + 2 * side - 1,
            me_c,
        )

    for side in range(2):

        @pl.when(has[2 + side])
        def _():
            edge_copy(side).start()

    for side in range(2):

        @pl.loop(0, comps // 8)
        def _(i):
            rows_of = [wave[pl.ds(i * 256 + j * 32 + side * 24, 8), :] for j in range(8)]
            outer = jnp.concatenate(rows_of, axis=0).astype(BF16)
            faces[side, pl.ds(pl.multiple_of(i * 64, 64), 64), :] = outer

    remote(near, near, near_send, near_recv, me_r, after * span + me_n).wait_recv()

    cut = span // 2

    def whole(g):
        return pl.ds(g * span, span)

    def pass_on(k):
        first, second = (pl.ds(0, cut), pl.ds(cut, span - cut))
        source, target_at, group = [
            (near.at[across, first], relay.at[first], after),
            (near.at[across, second], relay.at[second], before),
            (near.at[after], traces.at[me_r, whole(mine)], after),
            (near.at[before], traces.at[me_r, whole(mine)], before),
            (relay.at[first], traces.at[me_r, pl.ds(before * span, cut)], after),
            (relay.at[second], traces.at[me_r, pl.ds(after * span + cut, span - cut)], before),
        ][k]
        return remote(
            source, target_at, pass_send.at[k], pass_recv.at[k], me_r, group * span + me_n
        )

    def passed(k):
        first, second = (pl.ds(0, cut), pl.ds(cut, span - cut))
        ref, group = [
            (relay.at[first], before),
            (relay.at[second], after),
            (traces.at[me_r, whole(before)], before),
            (traces.at[me_r, whole(after)], after),
            (traces.at[me_r, pl.ds(across * span, cut)], before),
            (traces.at[me_r, pl.ds(across * span + cut, span - cut)], after),
        ][k]
        return remote(ref, ref, pass_send.at[k], pass_recv.at[k], me_r, group * span + me_n)

    halves = [k for k in (0, 1) if k == 1 or cut > 0]
    for k in halves:
        pass_on(k).start()
    pass_on(2).start()
    pass_on(3).start()
    own_group = pltpu.make_async_copy(near.at[mine], traces.at[me_r, whole(mine)], own_sem)
    own_group.start()

    wide = rows // 2

    def row_at(dz, dx):
        return (me_r // wide + dz) % 2 * wide + (me_r % wide + dx) % wide

    across_x = wide // 2
    steps = [(0, across_x), (0, 1), (0, wide - 1), (1, 0)] if wide > 1 else [(1, 0)]
    far_steps = [(1, across_x), (1, 1), (1, wide - 1)] if wide > 1 else []
    plane, opposite = row_at(1, 0), row_at(0, across_x)

    def row_copy(k, step, g, r, source):
        return remote(
            source, traces.at[r, whole(g)], row_send.at[k, g], row_recv.at[r, g], row_at(*step), me_c
        )

    def row_arrival(r, g):
        ref = traces.at[r, whole(g)]
        return remote(ref, ref, row_send.at[0, g], row_recv.at[r, g], plane, me_c)

    def first_hops(g, source):
        return [row_copy(k, step, g, me_r, source) for k, step in enumerate(steps)]

    def second_hops(g, first, last):
        sends = [(4, (0, 1), plane), (5, (0, wide - 1), plane), (6, (1, 0), opposite)]
        return [
            row_copy(k, step, g, r, traces.at[r, whole(g)])
            for k, step, r in (sends[first:last] if wide > 1 else [])
        ]

    def far_hops(g, source):
        return [row_copy(4 + k, step, g, me_r, source) for k, step in enumerate(far_steps)]

    def go(copies):
        for copy in copies:
            copy.start()

    def go_on(g):
        if wide > 1:
            row_arrival(plane, g).wait_recv()
            go(second_hops(g, 0, 2))
            row_arrival(opposite, g).wait_recv()
            go(second_hops(g, 2, 3))

    go(first_hops(mine, near.at[mine]))

    loads[3].wait()

    @pl.loop(0, comps // 8)
    def _(i):
        start = pl.multiple_of(i * 256, 256)
        wide = jnp.where(here[None], flux[pl.ds(i * 8, 8), :, :], 0.0).reshape(256, nodes)
        upper = wide.astype(BF16)
        lower = (wide - upper.astype(F32)).astype(BF16)
        volume[pl.ds(start, 256), :] = nt_dot(upper, onehot[...]) + nt_dot(lower, onehot[...])

    for k in halves:
        passed(k).wait_recv()
        pass_on(4 + k).start()

    for k, g in ((2, before), (3, after)):
        passed(k).wait_recv()
        go(first_hops(g, traces.at[me_r, whole(g)]))

    go_on(mine)

    packed_rows = cols // 2 * 8
    window, shift = nodes * 2 // 3, nodes // 6
    at_row = iota((window, packed_rows), 0)
    packed = iota((window, packed_rows), 1)
    for part in range(2):
        for half in range(2):
            hit = jnp.logical_and(
                at_row - part * shift == (packed // 8) * slot_len + packed % 8 + half * half_slot,
                packed % 8 < half_slot,
            )
            unpack[part, :, half * packed_rows : (half + 1) * packed_rows] = jnp.where(
                hit, 1.0, 0.0
            ).astype(BF16)
    total[...] = jnp.zeros_like(total)

    for k in halves:
        passed(4 + k).wait_recv()
    go(far_hops(across, traces.at[me_r, whole(across)]))
    go(first_hops(across, traces.at[me_r, whole(across)]))
    go_on(before)
    go_on(after)

    def face_copy(side):
        return remote(
            faces.at[side],
            faces_in.at[1 - side],
            halo_send.at[side],
            halo_recv.at[side],
            me_r,
            me_c + 2 * side - 1,
        )

    for side in range(2):

        @pl.when(has[side])
        def _():
            face_copy(side).start()

    def corner_copy(side, way):
        return remote(
            edges_in.at[side, 3 * way],
            corners_in.at[2 - 2 * way + side],
            halo_send.at[4 + 2 * side + way],
            halo_recv.at[4 + 2 * side + way],
            me_r,
            me_c + 2 * way - 1,
        )

    for side in range(2):

        @pl.when(has[2 + side])
        def _():
            ref = edges_in.at[side]
            remote(
                ref, ref, halo_send.at[3 - side], halo_recv.at[3 - side], me_r + 2 * side - 1, me_c
            ).wait_recv()
            for way in range(2):

                @pl.when(has[way])
                def _():
                    corner_copy(side, way).start()

    own_group.wait()
    loads[5].wait()
    left = iota((packed_rows, 128), 1) < comps
    minus = iota((packed_rows, 128), 1) % comps < comps // 2
    slab = matrix.shape[1]
    for late in range(2):
        part = (mine // 2 + late) % 2

        def arrivals(step, g):
            row_arrival(row_at(*step), g).wait_recv()

        for step in steps + far_steps:
            if late:
                arrivals(step, across)
                if step not in ((1, 0), (0, across_x)) or wide == 1:
                    arrivals(step, jnp.where(mine % 2 == 0, before, after))
            elif step not in ((1, 0), (0, across_x)) or wide == 1:
                arrivals(step, mine)
                arrivals(step, jnp.where(mine % 2 == 0, after, before))

        for r in range(rows):
            raw = traces[r, pl.ds(part * (cols // 2), cols // 2)]
            raw = raw.reshape(packed_rows, 2 * comps).astype(F32)
            turned = pltpu.roll(raw, comps, 1)
            stacked = []
            for half in range(2):
                same = jnp.where(left, raw, turned) if half == 0 else jnp.where(left, turned, raw)
                swapped = pltpu.roll(same, comps // 2, 1)
                swapped = jnp.where(minus, -swapped, swapped)
                stacked.append(jnp.concatenate([same, swapped], axis=1).astype(BF16))
            both = nn_dot(unpack[part], jnp.concatenate(stacked, axis=0))
            placed[r] = both.astype(BF16)

        @pl.loop(0, 2)
        def _(i):
            upright = pl.ds(pl.multiple_of(i * (slab // 2), slab // 2), slab // 2)
            terms = total[upright, :]
            for r in range(rows):
                at = r * nodes + part * (nodes // 3)
                columns = pl.ds(pl.multiple_of(at, nodes // 3), window)
                for half in range(2):
                    terms += nn_dot(
                        matrix[half, upright, columns], placed[r, :, half * 128 : half * 128 + 128]
                    )
            total[upright, :] = terms

    tiles = total[...].reshape(cols, 2, 8, 128)
    parts[...] = jnp.where(
        iota((cols, 8, 128), 2) < comps, tiles[:, 0], tiles[:, 1]
    ).astype(BF16)

    def part_copy(t, source):
        return remote(
            parts.at[t], landed.at[source], part_send, part_recv, me_r, t
        )

    for hop in (2, 1, 3, 0):
        first = ((mine + hop) % GROUPS) * span

        @pl.loop(0, span)
        def _(i):
            t = first + i

            @pl.when(t != me_c)
            def _():
                part_copy(t, me_c).start()

    own_part = pltpu.make_async_copy(parts.at[me_c], landed.at[me_c], part_recv)
    own_part.start()

    halos = [
        (faces_in.at[1 - side], faces_f.at[1 - side], side, has[1 - side], (0, 1 - 2 * side))
        for side in range(2)
    ]
    halos += [
        (edges_in.at[side], edges_f.at[side], -1, has[2 + side], None) for side in range(2)
    ]
    halos += [
        (
            corners_in.at[2 - 2 * way + side],
            corners_f.at[2 - 2 * way + side],
            4 + 2 * side + way,
            jnp.logical_and(has[1 - way], has[2 + side]),
            (0, 1 - 2 * way),
        )
        for side in range(2)
        for way in range(2)
    ]
    for got, kept, k, there, step in halos:

        @pl.when(there)
        def _():
            if step is not None:
                remote(
                    got, got, halo_send.at[k], halo_recv.at[k], me_r + step[0], me_c + step[1]
                ).wait_recv()
            kept[...] = got[...].astype(F32)

        @pl.when(jnp.logical_not(there))
        def _():
            kept[...] = jnp.zeros(kept.shape, F32)

    loads[4].wait()
    sublane = iota((8, 128), 0)
    lane = iota((8, 128), 1)

    def depth_sides(v):
        below = jnp.where(lane == 0, 0.0, pltpu.roll(v, 1, 1))
        above = jnp.where(lane == 127, 0.0, pltpu.roll(v, 127, 1))
        return below + above

    def layer(u, low, high):
        below = jnp.where(sublane == 0, jnp.broadcast_to(low, (8, 128)), pltpu.roll(u, 1, 0))
        above = jnp.where(sublane == 7, jnp.broadcast_to(high, (8, 128)), pltpu.roll(u, 7, 0))
        sides = below + above
        outer = depth_sides(sides)
        ring = 2.0 * (sides + depth_sides(u)) + outer
        return u, outer, ring, 4.0 * u + ring

    @pl.loop(0, comps, unroll=4)
    def _(k):
        layers = []
        for x in range(6):
            if x in (0, 5):
                side = 0 if x == 0 else 1
                u = faces_f[side, pl.ds(pl.multiple_of(k * 8, 8), 8), :]
                low = corners_f[2 * side, pl.ds(k, 1), :]
                high = corners_f[2 * side + 1, pl.ds(k, 1), :]
            else:
                u = wave[pl.ds(pl.multiple_of(k * 32 + (x - 1) * 8, 8), 8), :]
                low = edges_f[0, x - 1, pl.ds(k, 1), :]
                high = edges_f[1, x - 1, pl.ds(k, 1), :]
            layers.append(layer(u, low, high))
        for x in range(1, 5):
            u, outer, ring, mass = layers[x]
            stiffness = (8.0 / 3.0) * u - (1.0 / 6.0) * outer
            stiffness -= (1.0 / 12.0) * (layers[x - 1][2] + layers[x + 1][2])
            mass_sum = (2.0 * mass + (layers[x - 1][3] + layers[x + 1][3])) * (1.0 / 27.0)
            where = pl.ds(pl.multiple_of(k * 32 + (x - 1) * 8, 8), 8)
            volume[where, :] = (
                stiffness - medium[pl.ds((x - 1) * 8, 8), :] * mass_sum - volume[where, :]
            )

    if span > 1:
        others = slots.at[pl.ds(0, span - 1)]
        remote(others, others, near_send, near_recv, me_r, after * span + me_n).wait_send()

    for k in halves:
        pass_on(k).wait_send()
        pass_on(4 + k).wait_send()
    pass_on(2).wait_send()
    pass_on(3).wait_send()

    for g in (mine, before, after, across):
        for copy in first_hops(g, traces.at[me_r, whole(g)]):
            copy.wait_send()
    for g in (mine, before, after):
        for copy in second_hops(g, 0, 3):
            copy.wait_send()
    for copy in far_hops(across, traces.at[me_r, whole(across)]):
        copy.wait_send()

    for side in range(2):

        @pl.when(has[side])
        def _():
            face_copy(side).wait_send()

        @pl.when(has[2 + side])
        def _():
            edge_copy(side).wait_send()
            for way in range(2):

                @pl.when(has[way])
                def _():
                    corner_copy(side, way).wait_send()

    remote(landed, landed, part_send, part_recv, me_r, after * span + me_n).wait_recv()

    sums = jnp.sum(landed[...].astype(F32), axis=0)
    boundary_out[0:8, :] = sums[:, :comps]
    boundary_out[8:16, :] = pltpu.roll(sums, comps, 1)[:, :comps]

    others = parts.at[pl.ds(0, cols - 1)]
    remote(others, others, part_send, part_recv, me_r, after * span + me_n).wait_send()


def on_device(rows, cols, wave_field, medium_term, node_flux, node_cell, block_target, boundary_matrix):
    comps = wave_field.shape[0]
    nodes = node_cell.shape[-1]
    slab_rows, width = boundary_matrix.shape[1:]
    own_rows = slab_rows // cols
    vmem = pltpu.VMEM
    dma = pltpu.SemaphoreType.DMA
    volume, boundary = pl.pallas_call(
        functools.partial(kernel, rows, cols),
        out_shape=(
            pltpu.VMEM((comps * 32, 128), F32),
            pltpu.VMEM((own_rows, comps), F32),
        ),
        in_specs=[pl.BlockSpec(memory_space=pltpu.HBM)] * 6,
        out_specs=(pl.BlockSpec(memory_space=pltpu.VMEM), pl.BlockSpec(memory_space=pltpu.VMEM)),
        scratch_shapes=[
            vmem((comps * 32, 128), F32),
            vmem((32, 128), F32),
            vmem((comps, 1, nodes), F32),
            vmem((1, nodes), jnp.int32),
            vmem((1, cols), jnp.int32),
            vmem((2, slab_rows, width), BF16),
            vmem((128, nodes), BF16),
            vmem((comps * 8, nodes), BF16),
            vmem((2, nodes * 2 // 3, cols * 8), BF16),
            vmem((rows, nodes * 2 // 3, 256), BF16),
            vmem((cols // GROUPS, GROUPS, 8, 128), BF16),
            vmem((GROUPS, cols // GROUPS, 8, 128), BF16),
            vmem((cols // GROUPS, 8, 128), BF16),
            vmem((rows, cols, 8, 128), BF16),
            vmem((slab_rows, 128), F32),
            vmem((cols, 8, 128), BF16),
            vmem((cols, 8, 128), BF16),
            vmem((2, comps * 8, 128), BF16),
            vmem((2, 4, comps, 128), BF16),
            vmem((2, comps * 8, 128), BF16),
            vmem((2, 4, comps, 128), BF16),
            vmem((4, comps, 128), BF16),
            vmem((2, comps * 8, 128), F32),
            vmem((2, 4, comps, 128), F32),
            vmem((4, comps, 128), F32),
            dma((6,)),
            dma(()),
            dma(()),
            dma((6,)),
            dma((6,)),
            dma(()),
            dma((7, GROUPS)),
            dma((rows, GROUPS)),
            dma(()),
            dma(()),
            dma((8,)),
            dma((8,)),
        ],
        compiler_params=pltpu.CompilerParams(
            collective_id=0, has_side_effects=True, vmem_limit_bytes=48 * 2**20
        ),
        name="coupled_apply",
    )(
        *[
            pltpu.with_memory_space_constraint(x, pltpu.HBM)
            for x in (
                wave_field.reshape(comps * 32, 128),
                medium_term.reshape(32, 128),
                node_flux.reshape(comps, 1, nodes),
                node_cell.reshape(1, nodes),
                block_target.reshape(1, cols),
                boundary_matrix,
            )
        ]
    )
    return volume.reshape(wave_field.shape), boundary


def solution(mesh):
    in_specs = (
        P(None, "col", "row", None),
        P("col", "row", None),
        P(None, "col", "row", None),
        P("col", "row", None),
        P("col", "row", None),
        P(None, "row", "col"),
    )
    out_specs = (P(None, "col", "row", None), P(("row", "col"), None))
    return jax.shard_map(
        functools.partial(on_device, mesh.shape["row"], mesh.shape["col"]),
        mesh=mesh,
        in_specs=in_specs,
        out_specs=out_specs,
        check_vma=False,
    )
```

```python
import functools

import jax
import jax.numpy as jnp
from jax import lax
from jax.experimental import pallas as pl
from jax.experimental.pallas import tpu as pltpu
from jax.sharding import PartitionSpec as P

MESH = pl.DeviceIdType.MESH
F32 = jnp.float32
BF16 = jnp.bfloat16
GROUPS = 4


def iota(shape, dim):
    return lax.broadcasted_iota(jnp.int32, shape, dim)


def nt_dot(a, b):
    return lax.dot_general(a, b, (((1,), (1,)), ((), ())), preferred_element_type=F32)


def nn_dot(a, b):
    return lax.dot_general(a, b, (((1,), (0,)), ((), ())), preferred_element_type=F32)


def kernel(
    rows, cols,
    wave_in, medium_in, flux_in, cell_in, target_in, matrix_in,
    volume, boundary_out,
    wave, medium, flux, cell, target, matrix, onehot, picked, order_of, placed, slots, near, outgoing, traces,
    total, parts, landed,
    faces, edges, faces_in, edges_in, corners_in, faces_f, edges_f, corners_f,
    in_sem, ready, near_send, near_recv, pass_send, pass_recv, row_send, row_recv, part_send, part_recv,
    halo_send, halo_recv,
):
    me_r = lax.axis_index("row")
    me_c = lax.axis_index("col")
    comps = wave.shape[0] // 32
    nodes = cell.shape[1]
    slot_len = nodes // cols
    half_slot = slot_len // 2
    span = cols // GROUPS
    mine = me_c // span
    me_n = me_c % span
    after, across, before = [(mine + d) % GROUPS for d in (1, 2, 3)]

    loads = [
        pltpu.make_async_copy(src, dst, in_sem.at[i])
        for i, (src, dst) in enumerate(
            [
                (cell_in, cell),
                (target_in, target),
                (wave_in, wave),
                (flux_in, flux),
                (medium_in, medium),
                (matrix_in, matrix),
            ]
        )
    ]
    for load in loads:
        load.start()

    barrier = pltpu.get_barrier_semaphore()

    def greet(r, c):
        pl.semaphore_signal(barrier, inc=1, device_id=(r, c), device_id_type=MESH)

    greet(me_r, after * span + me_n)
    greet(me_r, before * span + me_n)

    @pl.loop(1, rows)
    def _(i):
        greet((me_r + i) % rows, me_c)

    @pl.loop(1, span)
    def _(i):
        greet(me_r, mine * span + (me_n + i) % span)

    def remote(src, dst, send_sem, recv_sem, r, c):
        return pltpu.make_async_remote_copy(
            src_ref=src,
            dst_ref=dst,
            send_sem=send_sem,
            recv_sem=recv_sem,
            device_id=(r, c),
            device_id_type=MESH,
        )

    loads[0].wait()
    loads[1].wait()
    cells = cell[...]
    place = cells // 128
    onehot[...] = jnp.where(iota((128, nodes), 0) == cells % 128, 1.0, 0.0).astype(BF16)
    node = iota((1, nodes), 1)
    spread = jnp.where(iota((cols, nodes), 0) == iota((cols, nodes), 1) // slot_len, 1.0, 0.0)
    wanted = jnp.broadcast_to(target[...].astype(F32), (8, cols))
    wanted = nn_dot(wanted.astype(BF16), spread.astype(BF16))[:1].astype(jnp.int32)
    within = node % slot_len
    row_of = ((wanted % span) * GROUPS + wanted // span) * 8 + within % half_slot
    lane_half = within // half_slot

    loads[2].wait()
    here = iota((32, nodes), 0) == place

    @pl.loop(0, comps // 8, unroll=2)
    def _(i):
        start = pl.multiple_of(i * 256, 256)
        found = nn_dot(wave[pl.ds(start, 256), :].astype(BF16), onehot[...])
        found = jnp.where(here[None], found.reshape(8, 32, nodes), 0.0)
        found = found.reshape(8, 4, 8, nodes)
        found = (found[:, 0] + found[:, 1]) + (found[:, 2] + found[:, 3])
        picked[pl.ds(pl.multiple_of(i * 64, 64), 64), :] = found.reshape(64, nodes).astype(BF16)

    gather = jnp.where(iota((comps, comps * 8), 0) == iota((comps, comps * 8), 1) // 8, 1.0, 0.0)
    trace = nn_dot(gather.astype(BF16), picked[...])
    blank = jnp.zeros_like(trace)
    sent = None
    for half in range(2):
        match = jnp.logical_and(iota((cols * 8, nodes), 0) == row_of, lane_half == half)
        order = jnp.where(match, 1.0, 0.0).astype(BF16)
        pair = [trace, blank] if half == 0 else [blank, trace]
        term = nt_dot(order, jnp.concatenate(pair, axis=0).astype(BF16))
        sent = term if sent is None else sent + term
    slots[...] = sent.reshape(span, GROUPS, 8, 2 * comps).astype(BF16)

    pl.semaphore_wait(barrier, span - 1 + 2 + rows - 1)

    for group in (after, before):
        pl.semaphore_signal(
            ready, inc=1, device_id=(me_r, group * span + me_n), device_id_type=MESH
        )

    def near_copy(n, source):
        return remote(
            slots.at[n], near.at[:, source], near_send, near_recv, me_r, mine * span + n
        )

    @pl.loop(1, span)
    def _(i):
        near_copy((me_n + span - i) % span, me_n).start()

    own_slots = pltpu.make_async_copy(slots.at[me_n], near.at[:, me_n], near_recv)
    own_slots.start()

    has = [me_c > 0, me_c < cols - 1, me_r > 0, me_r < rows - 1]
    for side in range(2):
        for x in range(4):
            edges[side, x] = wave[pl.ds(x * 8 + side * 7, comps, stride=32), :].astype(BF16)

    def edge_copy(side):
        return remote(
            edges.at[side],
            edges_in.at[1 - side],
            halo_send.at[2 + side],
            halo_recv.at[2 + side],
            me_r + 2 * side - 1,
            me_c,
        )

    for side in range(2):

        @pl.when(has[2 + side])
        def _():
            edge_copy(side).start()

    for side in range(2):

        @pl.loop(0, comps // 8)
        def _(i):
            rows_of = [wave[pl.ds(i * 256 + j * 32 + side * 24, 8), :] for j in range(8)]
            outer = jnp.concatenate(rows_of, axis=0).astype(BF16)
            faces[side, pl.ds(pl.multiple_of(i * 64, 64), 64), :] = outer

    group_half = span * half_slot
    at_row = iota((2 * group_half, span * 16), 0)
    packed = iota((2 * group_half, span * 16), 1)
    turned_in = packed // (span * 8)
    upper_out = at_row // group_half
    from_node = packed % (span * 8) // 8 * slot_len + packed % 8
    from_node += jnp.where(turned_in == upper_out, 0, half_slot)
    hit = jnp.logical_and(from_node == at_row, packed % 8 < half_slot)
    order_of[...] = jnp.where(hit, 1.0, 0.0).astype(BF16)
    remote(near, near, near_send, near_recv, me_r, after * span + me_n).wait_recv()

    raw = [near[g].reshape(span * 8, 2 * comps) for g in range(GROUPS)]
    turned = [pltpu.roll(block.astype(F32), comps, 1).astype(BF16) for block in raw]
    stacks = [jnp.concatenate(pair, axis=0) for pair in zip(raw, turned)]
    found = nn_dot(order_of[...], jnp.concatenate(stacks, axis=1))
    found = jnp.where(
        iota((group_half, GROUPS * 128), 1) % 128 < comps, found[:group_half], found[group_half:]
    )
    piece = outgoing.shape[1:]
    for g in range(GROUPS):
        outgoing[g] = found[:, g * 128 : g * 128 + 128].reshape(piece).astype(BF16)

    beside = [across, after, before]

    def pass_on(k):
        return remote(
            outgoing.at[beside[k]],
            traces.at[me_r, mine],
            pass_send.at[k],
            pass_recv.at[k],
            me_r,
            beside[k] * span + me_n,
        )

    def passed(k):
        group = [across, before, after][k]
        ref = traces.at[me_r, group]
        return remote(ref, ref, pass_send.at[k], pass_recv.at[k], me_r, group * span + me_n)

    pl.semaphore_wait(ready, 2)
    for k in range(3):
        pass_on(k).start()
    traces[me_r, mine] = outgoing[mine]

    wide = rows // 2

    def row_at(dz, dx):
        return (me_r // wide + dz) % 2 * wide + (me_r % wide + dx) % wide

    across_x = wide // 2
    steps = [(0, across_x), (0, 1), (0, wide - 1), (1, 0)] if wide > 1 else [(1, 0)]
    far_steps = [(1, across_x), (1, 1), (1, wide - 1)] if wide > 1 else []
    plane, opposite = row_at(1, 0), row_at(0, across_x)

    def row_copy(k, step, g, r):
        ref = traces.at[r, g]
        return remote(ref, ref, row_send.at[k, g], row_recv.at[r, g], row_at(*step), me_c)

    def row_arrival(r, g):
        ref = traces.at[r, g]
        return remote(ref, ref, row_send.at[0, g], row_recv.at[r, g], plane, me_c)

    def first_hops(g):
        return [row_copy(k, step, g, me_r) for k, step in enumerate(steps)]

    def second_hops(g, first, last):
        sends = [(4, (0, 1), plane), (5, (0, wide - 1), plane), (6, (1, 0), opposite)]
        return [row_copy(k, step, g, r) for k, step, r in (sends[first:last] if wide > 1 else [])]

    def far_hops(g):
        return [row_copy(4 + k, step, g, me_r) for k, step in enumerate(far_steps)]

    def go(copies):
        for copy in copies:
            copy.start()

    def go_on(g):
        if wide > 1:
            row_arrival(plane, g).wait_recv()
            go(second_hops(g, 0, 2))
            row_arrival(opposite, g).wait_recv()
            go(second_hops(g, 2, 3))

    go(first_hops(mine))

    loads[3].wait()

    @pl.loop(0, comps // 8, unroll=2)
    def _(i):
        start = pl.multiple_of(i * 256, 256)
        wide = jnp.where(here[None], flux[pl.ds(i * 8, 8), :, :], 0.0).reshape(256, nodes)
        upper = wide.astype(BF16)
        lower = (wide - upper.astype(F32)).astype(BF16)
        volume[pl.ds(start, 256), :] = nt_dot(upper, onehot[...]) + nt_dot(lower, onehot[...])

    for k, g in ((1, before), (2, after)):
        passed(k).wait_recv()
        go(first_hops(g))

    total[...] = jnp.zeros_like(total)
    go_on(mine)
    passed(0).wait_recv()
    go(far_hops(across))
    go(first_hops(across))
    go_on(before)
    go_on(after)

    def face_copy(side):
        return remote(
            faces.at[side],
            faces_in.at[1 - side],
            halo_send.at[side],
            halo_recv.at[side],
            me_r,
            me_c + 2 * side - 1,
        )

    for side in range(2):

        @pl.when(has[side])
        def _():
            face_copy(side).start()

    def corner_copy(side, way):
        return remote(
            edges_in.at[side, 3 * way],
            corners_in.at[2 - 2 * way + side],
            halo_send.at[4 + 2 * side + way],
            halo_recv.at[4 + 2 * side + way],
            me_r,
            me_c + 2 * way - 1,
        )

    for side in range(2):

        @pl.when(has[2 + side])
        def _():
            ref = edges_in.at[side]
            remote(
                ref, ref, halo_send.at[3 - side], halo_recv.at[3 - side], me_r + 2 * side - 1, me_c
            ).wait_recv()
            for way in range(2):

                @pl.when(has[way])
                def _():
                    corner_copy(side, way).start()

    loads[5].wait()
    slab = matrix.shape[1]
    window, shift = nodes * 2 // 3, nodes // 6
    for late in range(2):
        part = (mine // 2 + late) % 2

        def arrivals(step, g):
            row_arrival(row_at(*step), g).wait_recv()

        for step in steps + far_steps:
            if late:
                arrivals(step, across)
                if step not in ((1, 0), (0, across_x)) or wide == 1:
                    arrivals(step, jnp.where(mine % 2 == 0, before, after))
            elif step not in ((1, 0), (0, across_x)) or wide == 1:
                arrivals(step, mine)
                arrivals(step, jnp.where(mine % 2 == 0, after, before))

        for r in range(rows):
            pieces = []
            for g in range(2):
                block = traces[r, 2 * part + g].astype(F32).reshape(group_half, 2 * comps)
                pieces += [block, pltpu.roll(block, comps, 1)]
            placed[r, pl.ds(pl.multiple_of(part * shift, shift), nodes // 2), :] = jnp.concatenate(
                pieces, axis=0
            ).astype(BF16)
            placed[r, pl.ds(pl.multiple_of((1 - part) * (nodes // 2), shift), shift), :] = (
                jnp.zeros((shift, 128), BF16)
            )

        @pl.loop(0, 2)
        def _(i):
            upright = pl.ds(pl.multiple_of(i * (slab // 2), slab // 2), slab // 2)
            for half in range(2):
                terms = total[half, upright, :]
                for r in range(rows):
                    at = r * nodes + part * (nodes // 3)
                    columns = pl.ds(pl.multiple_of(at, nodes // 3), window)
                    terms += nn_dot(matrix[half, upright, columns], placed[r])
                total[half, upright, :] = terms

    lower = iota((cols * 8, 128), 1) < comps
    minus = iota((cols * 8, 128), 1) % comps < comps // 2
    folded = []
    for half in range(2):
        tiles = total[half].reshape(cols, 2, 8, 128)
        first, second = [tiles[:, i].reshape(cols * 8, 128) for i in range(2)]
        folded.append(jnp.where(lower, first, pltpu.roll(second, comps, 1)))
    real, imag = folded
    imag = jnp.where(
        minus, -pltpu.roll(imag, 128 - comps // 2, 1), pltpu.roll(imag, comps // 2, 1)
    )
    parts[...] = (real + imag).reshape(cols, 8, 128).astype(BF16)

    def part_copy(t, source):
        return remote(
            parts.at[t], landed.at[source], part_send, part_recv, me_r, t
        )

    for hop in (2, 1, 3, 0):
        first = ((mine + hop) % GROUPS) * span

        @pl.loop(0, span)
        def _(i):
            t = first + i

            @pl.when(t != me_c)
            def _():
                part_copy(t, me_c).start()

    own_part = pltpu.make_async_copy(parts.at[me_c], landed.at[me_c], part_recv)
    own_part.start()

    halos = [
        (faces_in.at[1 - side], faces_f.at[1 - side], side, has[1 - side], (0, 1 - 2 * side))
        for side in range(2)
    ]
    halos += [
        (edges_in.at[side], edges_f.at[side], -1, has[2 + side], None) for side in range(2)
    ]
    halos += [
        (
            corners_in.at[2 - 2 * way + side],
            corners_f.at[2 - 2 * way + side],
            4 + 2 * side + way,
            jnp.logical_and(has[1 - way], has[2 + side]),
            (0, 1 - 2 * way),
        )
        for side in range(2)
        for way in range(2)
    ]
    for got, kept, k, there, step in halos:

        @pl.when(there)
        def _():
            if step is not None:
                remote(
                    got, got, halo_send.at[k], halo_recv.at[k], me_r + step[0], me_c + step[1]
                ).wait_recv()
            kept[...] = got[...].astype(F32)

        @pl.when(jnp.logical_not(there))
        def _():
            kept[...] = jnp.zeros(kept.shape, F32)

    loads[4].wait()
    sublane = iota((8, 128), 0)
    lane = iota((8, 128), 1)

    def depth_sides(v):
        below = jnp.where(lane == 0, 0.0, pltpu.roll(v, 1, 1))
        above = jnp.where(lane == 127, 0.0, pltpu.roll(v, 127, 1))
        return below + above

    def layer(u, low, high):
        below = jnp.where(sublane == 0, jnp.broadcast_to(low, (8, 128)), pltpu.roll(u, 1, 0))
        above = jnp.where(sublane == 7, jnp.broadcast_to(high, (8, 128)), pltpu.roll(u, 7, 0))
        sides = below + above
        outer = depth_sides(sides)
        ring = 2.0 * (sides + depth_sides(u)) + outer
        return u, outer, ring, 4.0 * u + ring

    @pl.loop(0, comps, unroll=4)
    def _(k):
        layers = []
        for x in range(6):
            if x in (0, 5):
                side = 0 if x == 0 else 1
                u = faces_f[side, pl.ds(pl.multiple_of(k * 8, 8), 8), :]
                low = corners_f[2 * side, pl.ds(k, 1), :]
                high = corners_f[2 * side + 1, pl.ds(k, 1), :]
            else:
                u = wave[pl.ds(pl.multiple_of(k * 32 + (x - 1) * 8, 8), 8), :]
                low = edges_f[0, x - 1, pl.ds(k, 1), :]
                high = edges_f[1, x - 1, pl.ds(k, 1), :]
            layers.append(layer(u, low, high))
        for x in range(1, 5):
            u, outer, ring, mass = layers[x]
            stiffness = (8.0 / 3.0) * u - (1.0 / 6.0) * outer
            stiffness -= (1.0 / 12.0) * (layers[x - 1][2] + layers[x + 1][2])
            mass_sum = (2.0 * mass + (layers[x - 1][3] + layers[x + 1][3])) * (1.0 / 27.0)
            where = pl.ds(pl.multiple_of(k * 32 + (x - 1) * 8, 8), 8)
            volume[where, :] = (
                stiffness - medium[pl.ds((x - 1) * 8, 8), :] * mass_sum - volume[where, :]
            )

    if span > 1:
        others = slots.at[pl.ds(0, span - 1)]
        remote(others, others, near_send, near_recv, me_r, after * span + me_n).wait_send()

    for k in range(3):
        pass_on(k).wait_send()

    for g in (mine, before, after, across):
        for copy in first_hops(g):
            copy.wait_send()
    for g in (mine, before, after):
        for copy in second_hops(g, 0, 3):
            copy.wait_send()
    for copy in far_hops(across):
        copy.wait_send()

    for side in range(2):

        @pl.when(has[side])
        def _():
            face_copy(side).wait_send()

        @pl.when(has[2 + side])
        def _():
            edge_copy(side).wait_send()
            for way in range(2):

                @pl.when(has[way])
                def _():
                    corner_copy(side, way).wait_send()

    remote(landed, landed, part_send, part_recv, me_r, after * span + me_n).wait_recv()

    sums = jnp.sum(landed[...].astype(F32), axis=0)
    boundary_out[0:8, :] = sums[:, :comps]
    boundary_out[8:16, :] = pltpu.roll(sums, comps, 1)[:, :comps]

    others = parts.at[pl.ds(0, cols - 1)]
    remote(others, others, part_send, part_recv, me_r, after * span + me_n).wait_send()


def on_device(rows, cols, wave_field, medium_term, node_flux, node_cell, block_target, boundary_matrix):
    comps = wave_field.shape[0]
    nodes = node_cell.shape[-1]
    slab_rows, width = boundary_matrix.shape[1:]
    own_rows = slab_rows // cols
    group_half = nodes // GROUPS // 2
    pieces = 6 if group_half % 48 == 0 else 2
    vmem = pltpu.VMEM
    dma = pltpu.SemaphoreType.DMA
    volume, boundary = pl.pallas_call(
        functools.partial(kernel, rows, cols),
        out_shape=(
            pltpu.VMEM((comps * 32, 128), F32),
            pltpu.VMEM((own_rows, comps), F32),
        ),
        in_specs=[pl.BlockSpec(memory_space=pltpu.HBM)] * 6,
        out_specs=(pl.BlockSpec(memory_space=pltpu.VMEM), pl.BlockSpec(memory_space=pltpu.VMEM)),
        scratch_shapes=[
            vmem((comps * 32, 128), F32),
            vmem((32, 128), F32),
            vmem((comps, 1, nodes), F32),
            vmem((1, nodes), jnp.int32),
            vmem((1, cols), jnp.int32),
            vmem((2, slab_rows, width), BF16),
            vmem((128, nodes), BF16),
            vmem((comps * 8, nodes), BF16),
            vmem((nodes // GROUPS, cols // GROUPS * 16), BF16),
            vmem((rows, nodes * 2 // 3, 128), BF16),
            vmem((cols // GROUPS, GROUPS, 8, 128), BF16),
            vmem((GROUPS, cols // GROUPS, 8, 128), BF16),
            vmem((GROUPS, pieces, group_half // pieces, 128), BF16),
            vmem((rows, GROUPS, pieces, group_half // pieces, 128), BF16),
            vmem((2, slab_rows, 128), F32),
            vmem((cols, 8, 128), BF16),
            vmem((cols, 8, 128), BF16),
            vmem((2, comps * 8, 128), BF16),
            vmem((2, 4, comps, 128), BF16),
            vmem((2, comps * 8, 128), BF16),
            vmem((2, 4, comps, 128), BF16),
            vmem((4, comps, 128), BF16),
            vmem((2, comps * 8, 128), F32),
            vmem((2, 4, comps, 128), F32),
            vmem((4, comps, 128), F32),
            dma((6,)),
            pltpu.SemaphoreType.REGULAR,
            dma(()),
            dma(()),
            dma((3,)),
            dma((3,)),
            dma((7, GROUPS)),
            dma((rows, GROUPS)),
            dma(()),
            dma(()),
            dma((8,)),
            dma((8,)),
        ],
        compiler_params=pltpu.CompilerParams(
            collective_id=0, has_side_effects=True, vmem_limit_bytes=48 * 2**20
        ),
        name="coupled_apply",
    )(
        *[
            pltpu.with_memory_space_constraint(x, pltpu.HBM)
            for x in (
                wave_field.reshape(comps * 32, 128),
                medium_term.reshape(32, 128),
                node_flux.reshape(comps, 1, nodes),
                node_cell.reshape(1, nodes),
                block_target.reshape(1, cols),
                boundary_matrix,
            )
        ]
    )
    return volume.reshape(wave_field.shape), boundary


def solution(mesh):
    in_specs = (
        P(None, "col", "row", None),
        P("col", "row", None),
        P(None, "col", "row", None),
        P("col", "row", None),
        P("col", "row", None),
        P(None, "row", "col"),
    )
    out_specs = (P(None, "col", "row", None), P(("row", "col"), None))
    return jax.shard_map(
        functools.partial(on_device, mesh.shape["row"], mesh.shape["col"]),
        mesh=mesh,
        in_specs=in_specs,
        out_specs=out_specs,
        check_vma=False,
    )
```

```python
import functools

import jax
import jax.numpy as jnp
from jax import lax
from jax.experimental import pallas as pl
from jax.experimental.pallas import tpu as pltpu
from jax.sharding import PartitionSpec as P

MESH = pl.DeviceIdType.MESH
F32 = jnp.float32
BF16 = jnp.bfloat16
GROUPS = 4


def iota(shape, dim):
    return lax.broadcasted_iota(jnp.int32, shape, dim)


def nt_dot(a, b):
    return lax.dot_general(a, b, (((1,), (1,)), ((), ())), preferred_element_type=F32)


def nn_dot(a, b):
    return lax.dot_general(a, b, (((1,), (0,)), ((), ())), preferred_element_type=F32)


def kernel(
    rows, cols,
    wave_in, medium_in, flux_in, cell_in, target_in, matrix_in,
    volume, boundary_out,
    wave, medium, flux, cell, target, matrix, onehot, picked, order_of, placed, slots, near, outgoing, traces,
    total, parts, landed,
    faces, edges, faces_in, edges_in, corners_in, faces_f, edges_f, corners_f,
    in_sem, ready, near_send, near_recv, pass_send, pass_recv, row_send, row_recv, part_send, part_recv,
    halo_send, halo_recv,
):
    me_r = lax.axis_index("row")
    me_c = lax.axis_index("col")
    comps = wave.shape[0] // 32
    nodes = cell.shape[1]
    slot_len = nodes // cols
    half_slot = slot_len // 2
    span = cols // GROUPS
    mine = me_c // span
    me_n = me_c % span
    after, across, before = [(mine + d) % GROUPS for d in (1, 2, 3)]

    loads = [
        pltpu.make_async_copy(src, dst, in_sem.at[i])
        for i, (src, dst) in enumerate(
            [
                (cell_in, cell),
                (target_in, target),
                (wave_in, wave),
                (flux_in, flux),
                (medium_in, medium),
                (matrix_in, matrix),
            ]
        )
    ]
    for load in loads:
        load.start()

    barrier = pltpu.get_barrier_semaphore()

    def greet(r, c):
        pl.semaphore_signal(barrier, inc=1, device_id=(r, c), device_id_type=MESH)

    greet(me_r, after * span + me_n)
    greet(me_r, before * span + me_n)

    @pl.loop(1, rows)
    def _(i):
        greet((me_r + i) % rows, me_c)

    @pl.loop(1, span)
    def _(i):
        greet(me_r, mine * span + (me_n + i) % span)

    def remote(src, dst, send_sem, recv_sem, r, c):
        return pltpu.make_async_remote_copy(
            src_ref=src,
            dst_ref=dst,
            send_sem=send_sem,
            recv_sem=recv_sem,
            device_id=(r, c),
            device_id_type=MESH,
        )

    loads[0].wait()
    loads[1].wait()
    cells = cell[...]
    place = cells // 128
    onehot[...] = jnp.where(iota((128, nodes), 0) == cells % 128, 1.0, 0.0).astype(BF16)
    node = iota((1, nodes), 1)
    spread = jnp.where(iota((cols, nodes), 0) == iota((cols, nodes), 1) // slot_len, 1.0, 0.0)
    wanted = jnp.broadcast_to(target[...].astype(F32), (8, cols))
    wanted = nn_dot(wanted.astype(BF16), spread.astype(BF16))[:1].astype(jnp.int32)
    within = node % slot_len
    row_of = ((wanted % span) * GROUPS + wanted // span) * 8 + within % half_slot
    lane_half = within // half_slot

    loads[2].wait()
    here = iota((32, nodes), 0) == place

    @pl.loop(0, comps // 8, unroll=2)
    def _(i):
        start = pl.multiple_of(i * 256, 256)
        found = nn_dot(wave[pl.ds(start, 256), :].astype(BF16), onehot[...])
        found = jnp.where(here[None], found.reshape(8, 32, nodes), 0.0)
        found = found.reshape(8, 4, 8, nodes)
        found = (found[:, 0] + found[:, 1]) + (found[:, 2] + found[:, 3])
        picked[pl.ds(pl.multiple_of(i * 64, 64), 64), :] = found.reshape(64, nodes).astype(BF16)

    gather = jnp.where(iota((comps, comps * 8), 0) == iota((comps, comps * 8), 1) // 8, 1.0, 0.0)
    trace = nn_dot(gather.astype(BF16), picked[...])
    blank = jnp.zeros_like(trace)
    sent = None
    for half in range(2):
        match = jnp.logical_and(iota((cols * 8, nodes), 0) == row_of, lane_half == half)
        order = jnp.where(match, 1.0, 0.0).astype(BF16)
        pair = [trace, blank] if half == 0 else [blank, trace]
        term = nt_dot(order, jnp.concatenate(pair, axis=0).astype(BF16))
        sent = term if sent is None else sent + term
    slots[...] = sent.reshape(span, GROUPS, 8, 2 * comps).astype(BF16)

    pl.semaphore_wait(barrier, span - 1 + 2 + rows - 1)

    for group in (after, before):
        pl.semaphore_signal(
            ready, inc=1, device_id=(me_r, group * span + me_n), device_id_type=MESH
        )

    def near_copy(n, source):
        return remote(
            slots.at[n], near.at[:, source], near_send, near_recv, me_r, mine * span + n
        )

    @pl.loop(1, span)
    def _(i):
        near_copy((me_n + span - i) % span, me_n).start()

    own_slots = pltpu.make_async_copy(slots.at[me_n], near.at[:, me_n], near_recv)
    own_slots.start()

    has = [me_c > 0, me_c < cols - 1, me_r > 0, me_r < rows - 1]
    for side in range(2):
        for x in range(4):
            edges[side, x] = wave[pl.ds(x * 8 + side * 7, comps, stride=32), :].astype(BF16)

    def edge_copy(side):
        return remote(
            edges.at[side],
            edges_in.at[1 - side],
            halo_send.at[2 + side],
            halo_recv.at[2 + side],
            me_r + 2 * side - 1,
            me_c,
        )

    for side in range(2):

        @pl.when(has[2 + side])
        def _():
            edge_copy(side).start()

    for side in range(2):

        @pl.loop(0, comps // 8)
        def _(i):
            rows_of = [wave[pl.ds(i * 256 + j * 32 + side * 24, 8), :] for j in range(8)]
            outer = jnp.concatenate(rows_of, axis=0).astype(BF16)
            faces[side, pl.ds(pl.multiple_of(i * 64, 64), 64), :] = outer

    group_half = span * half_slot
    at_row = iota((2 * group_half, span * 16), 0)
    packed = iota((2 * group_half, span * 16), 1)
    turned_in = packed // (span * 8)
    upper_out = at_row // group_half
    from_node = packed % (span * 8) // 8 * slot_len + packed % 8
    from_node += jnp.where(turned_in == upper_out, 0, half_slot)
    hit = jnp.logical_and(from_node == at_row, packed % 8 < half_slot)
    order_of[...] = jnp.where(hit, 1.0, 0.0).astype(BF16)
    remote(near, near, near_send, near_recv, me_r, after * span + me_n).wait_recv()

    raw = [near[g].reshape(span * 8, 2 * comps) for g in range(GROUPS)]
    turned = [pltpu.roll(block.astype(F32), comps, 1).astype(BF16) for block in raw]
    stacks = [jnp.concatenate(pair, axis=0) for pair in zip(raw, turned)]
    found = nn_dot(order_of[...], jnp.concatenate(stacks, axis=1))
    found = jnp.where(
        iota((group_half, GROUPS * 128), 1) % 128 < comps, found[:group_half], found[group_half:]
    )
    piece = outgoing.shape[1:]
    for g in range(GROUPS):
        outgoing[g] = found[:, g * 128 : g * 128 + 128].reshape(piece).astype(BF16)

    beside = [across, after, before]

    def pass_on(k):
        return remote(
            outgoing.at[beside[k]],
            traces.at[me_r, mine],
            pass_send.at[k],
            pass_recv.at[k],
            me_r,
            beside[k] * span + me_n,
        )

    def passed(k):
        group = [across, before, after][k]
        ref = traces.at[me_r, group]
        return remote(ref, ref, pass_send.at[k], pass_recv.at[k], me_r, group * span + me_n)

    pl.semaphore_wait(ready, 2)
    for k in range(3):
        pass_on(k).start()
    traces[me_r, mine] = outgoing[mine]

    wide = rows // 2

    def row_at(dz, dx):
        return (me_r // wide + dz) % 2 * wide + (me_r % wide + dx) % wide

    across_x = wide // 2
    steps = [(0, across_x), (0, 1), (0, wide - 1), (1, 0)] if wide > 1 else [(1, 0)]
    far_steps = [(1, across_x), (1, 1), (1, wide - 1)] if wide > 1 else []
    plane, opposite = row_at(1, 0), row_at(0, across_x)

    def row_copy(k, step, g, r):
        ref = traces.at[r, g]
        return remote(ref, ref, row_send.at[k, g], row_recv.at[r, g], row_at(*step), me_c)

    def row_arrival(r, g):
        ref = traces.at[r, g]
        return remote(ref, ref, row_send.at[0, g], row_recv.at[r, g], plane, me_c)

    def first_hops(g):
        return [row_copy(k, step, g, me_r) for k, step in enumerate(steps)]

    def second_hops(g, first, last):
        sends = [(4, (0, 1), plane), (5, (0, wide - 1), plane), (6, (1, 0), opposite)]
        return [row_copy(k, step, g, r) for k, step, r in (sends[first:last] if wide > 1 else [])]

    def far_hops(g):
        return [row_copy(4 + k, step, g, me_r) for k, step in enumerate(far_steps)]

    def go(copies):
        for copy in copies:
            copy.start()

    def go_on(g):
        if wide > 1:
            row_arrival(plane, g).wait_recv()
            go(second_hops(g, 0, 2))
            row_arrival(opposite, g).wait_recv()
            go(second_hops(g, 2, 3))

    go(first_hops(mine))

    loads[3].wait()

    @pl.loop(0, comps // 8, unroll=2)
    def _(i):
        start = pl.multiple_of(i * 256, 256)
        wide = jnp.where(here[None], flux[pl.ds(i * 8, 8), :, :], 0.0).reshape(256, nodes)
        upper = wide.astype(BF16)
        lower = (wide - upper.astype(F32)).astype(BF16)
        volume[pl.ds(start, 256), :] = nt_dot(upper, onehot[...]) + nt_dot(lower, onehot[...])

    for k, g in ((1, before), (2, after)):
        passed(k).wait_recv()
        go(far_hops(g))
        go(first_hops(g))

    total[...] = jnp.zeros_like(total)
    go_on(mine)
    passed(0).wait_recv()
    go(far_hops(across))
    go(first_hops(across))

    def face_copy(side):
        return remote(
            faces.at[side],
            faces_in.at[1 - side],
            halo_send.at[side],
            halo_recv.at[side],
            me_r,
            me_c + 2 * side - 1,
        )

    for side in range(2):

        @pl.when(has[side])
        def _():
            face_copy(side).start()

    def corner_copy(side, way):
        return remote(
            edges_in.at[side, 3 * way],
            corners_in.at[2 - 2 * way + side],
            halo_send.at[4 + 2 * side + way],
            halo_recv.at[4 + 2 * side + way],
            me_r,
            me_c + 2 * way - 1,
        )

    for side in range(2):

        @pl.when(has[2 + side])
        def _():
            ref = edges_in.at[side]
            remote(
                ref, ref, halo_send.at[3 - side], halo_recv.at[3 - side], me_r + 2 * side - 1, me_c
            ).wait_recv()
            for way in range(2):

                @pl.when(has[way])
                def _():
                    corner_copy(side, way).start()

    loads[5].wait()
    slab = matrix.shape[1]
    third = nodes // 3
    early = mine // 2
    for late in range(2):
        part = (mine // 2 + late) % 2

        def arrivals(step, g):
            row_arrival(row_at(*step), g).wait_recv()

        for step in steps + far_steps:
            if late:
                arrivals(step, across)
                arrivals(step, jnp.where(mine % 2 == 0, before, after))
            else:
                arrivals(step, jnp.where(mine % 2 == 0, after, before))
                if step not in ((1, 0), (0, across_x)) or wide == 1:
                    arrivals(step, mine)

        for r in range(rows):
            pieces = []
            for g in range(2):
                block = traces[r, 2 * part + g].astype(F32).reshape(group_half, 2 * comps)
                pieces += [block, pltpu.roll(block, comps, 1)]
            placed[r, pl.ds(pl.multiple_of(part * (nodes // 2), nodes // 2), nodes // 2), :] = (
                jnp.concatenate(pieces, axis=0).astype(BF16)
            )

        if late:
            first, width, joined = (1 - early) * third, 2 * third, 1
        else:
            first, width, joined = 2 * early * third, third, 2

        @pl.loop(0, 2)
        def _(i):
            upright = pl.ds(pl.multiple_of(i * (slab // 2), slab // 2), slab // 2)
            for half in range(2):
                terms = total[half, upright, :]
                for r in range(0, rows, joined):
                    lhs, rhs = [], []
                    for q in range(r, r + joined):
                        columns = pl.ds(pl.multiple_of(q * nodes + first, third), width)
                        lhs.append(matrix[half, upright, columns])
                        rhs.append(placed[q, pl.ds(pl.multiple_of(first, third), width), :])
                    terms += nn_dot(jnp.concatenate(lhs, axis=1), jnp.concatenate(rhs, axis=0))
                total[half, upright, :] = terms

    lower = iota((cols * 8, 128), 1) < comps
    minus = iota((cols * 8, 128), 1) % comps < comps // 2
    folded = []
    for half in range(2):
        tiles = total[half].reshape(cols, 2, 8, 128)
        first, second = [tiles[:, i].reshape(cols * 8, 128) for i in range(2)]
        folded.append(jnp.where(lower, first, pltpu.roll(second, comps, 1)))
    real, imag = folded
    imag = jnp.where(
        minus, -pltpu.roll(imag, 128 - comps // 2, 1), pltpu.roll(imag, comps // 2, 1)
    )
    parts[...] = (real + imag).reshape(cols, 8, 128).astype(BF16)

    def part_copy(t, source):
        return remote(
            parts.at[t], landed.at[source], part_send, part_recv, me_r, t
        )

    for hop in (2, 1, 3, 0):
        first = ((mine + hop) % GROUPS) * span

        @pl.loop(0, span)
        def _(i):
            t = first + i

            @pl.when(t != me_c)
            def _():
                part_copy(t, me_c).start()

    own_part = pltpu.make_async_copy(parts.at[me_c], landed.at[me_c], part_recv)
    own_part.start()

    halos = [
        (faces_in.at[1 - side], faces_f.at[1 - side], side, has[1 - side], (0, 1 - 2 * side))
        for side in range(2)
    ]
    halos += [
        (edges_in.at[side], edges_f.at[side], -1, has[2 + side], None) for side in range(2)
    ]
    halos += [
        (
            corners_in.at[2 - 2 * way + side],
            corners_f.at[2 - 2 * way + side],
            4 + 2 * side + way,
            jnp.logical_and(has[1 - way], has[2 + side]),
            (0, 1 - 2 * way),
        )
        for side in range(2)
        for way in range(2)
    ]
    for got, kept, k, there, step in halos:

        @pl.when(there)
        def _():
            if step is not None:
                remote(
                    got, got, halo_send.at[k], halo_recv.at[k], me_r + step[0], me_c + step[1]
                ).wait_recv()
            kept[...] = got[...].astype(F32)

        @pl.when(jnp.logical_not(there))
        def _():
            kept[...] = jnp.zeros(kept.shape, F32)

    loads[4].wait()
    sublane = iota((8, 128), 0)
    lane = iota((8, 128), 1)

    def depth_sides(v):
        below = jnp.where(lane == 0, 0.0, pltpu.roll(v, 1, 1))
        above = jnp.where(lane == 127, 0.0, pltpu.roll(v, 127, 1))
        return below + above

    def layer(u, low, high):
        below = jnp.where(sublane == 0, jnp.broadcast_to(low, (8, 128)), pltpu.roll(u, 1, 0))
        above = jnp.where(sublane == 7, jnp.broadcast_to(high, (8, 128)), pltpu.roll(u, 7, 0))
        sides = below + above
        outer = depth_sides(sides)
        ring = 2.0 * (sides + depth_sides(u)) + outer
        return u, outer, ring, 4.0 * u + ring

    @pl.loop(0, comps, unroll=4)
    def _(k):
        layers = []
        for x in range(6):
            if x in (0, 5):
                side = 0 if x == 0 else 1
                u = faces_f[side, pl.ds(pl.multiple_of(k * 8, 8), 8), :]
                low = corners_f[2 * side, pl.ds(k, 1), :]
                high = corners_f[2 * side + 1, pl.ds(k, 1), :]
            else:
                u = wave[pl.ds(pl.multiple_of(k * 32 + (x - 1) * 8, 8), 8), :]
                low = edges_f[0, x - 1, pl.ds(k, 1), :]
                high = edges_f[1, x - 1, pl.ds(k, 1), :]
            layers.append(layer(u, low, high))
        for x in range(1, 5):
            u, outer, ring, mass = layers[x]
            stiffness = (8.0 / 3.0) * u - (1.0 / 6.0) * outer
            stiffness -= (1.0 / 12.0) * (layers[x - 1][2] + layers[x + 1][2])
            mass_sum = (2.0 * mass + (layers[x - 1][3] + layers[x + 1][3])) * (1.0 / 27.0)
            where = pl.ds(pl.multiple_of(k * 32 + (x - 1) * 8, 8), 8)
            volume[where, :] = (
                stiffness - medium[pl.ds((x - 1) * 8, 8), :] * mass_sum - volume[where, :]
            )

    if span > 1:
        others = slots.at[pl.ds(0, span - 1)]
        remote(others, others, near_send, near_recv, me_r, after * span + me_n).wait_send()

    for k in range(3):
        pass_on(k).wait_send()

    for g in (mine, before, after, across):
        for copy in first_hops(g):
            copy.wait_send()
    for copy in second_hops(mine, 0, 3):
        copy.wait_send()
    for g in (before, after, across):
        for copy in far_hops(g):
            copy.wait_send()

    for side in range(2):

        @pl.when(has[side])
        def _():
            face_copy(side).wait_send()

        @pl.when(has[2 + side])
        def _():
            edge_copy(side).wait_send()
            for way in range(2):

                @pl.when(has[way])
                def _():
                    corner_copy(side, way).wait_send()

    remote(landed, landed, part_send, part_recv, me_r, after * span + me_n).wait_recv()

    sums = jnp.sum(landed[...].astype(F32), axis=0)
    boundary_out[0:8, :] = sums[:, :comps]
    boundary_out[8:16, :] = pltpu.roll(sums, comps, 1)[:, :comps]

    others = parts.at[pl.ds(0, cols - 1)]
    remote(others, others, part_send, part_recv, me_r, after * span + me_n).wait_send()


def on_device(rows, cols, wave_field, medium_term, node_flux, node_cell, block_target, boundary_matrix):
    comps = wave_field.shape[0]
    nodes = node_cell.shape[-1]
    slab_rows, width = boundary_matrix.shape[1:]
    own_rows = slab_rows // cols
    group_half = nodes // GROUPS // 2
    pieces = 6 if group_half % 48 == 0 else 2
    vmem = pltpu.VMEM
    dma = pltpu.SemaphoreType.DMA
    volume, boundary = pl.pallas_call(
        functools.partial(kernel, rows, cols),
        out_shape=(
            pltpu.VMEM((comps * 32, 128), F32),
            pltpu.VMEM((own_rows, comps), F32),
        ),
        in_specs=[pl.BlockSpec(memory_space=pltpu.HBM)] * 6,
        out_specs=(pl.BlockSpec(memory_space=pltpu.VMEM), pl.BlockSpec(memory_space=pltpu.VMEM)),
        scratch_shapes=[
            vmem((comps * 32, 128), F32),
            vmem((32, 128), F32),
            vmem((comps, 1, nodes), F32),
            vmem((1, nodes), jnp.int32),
            vmem((1, cols), jnp.int32),
            vmem((2, slab_rows, width), BF16),
            vmem((128, nodes), BF16),
            vmem((comps * 8, nodes), BF16),
            vmem((nodes // GROUPS, cols // GROUPS * 16), BF16),
            vmem((rows, nodes, 128), BF16),
            vmem((cols // GROUPS, GROUPS, 8, 128), BF16),
            vmem((GROUPS, cols // GROUPS, 8, 128), BF16),
            vmem((GROUPS, pieces, group_half // pieces, 128), BF16),
            vmem((rows, GROUPS, pieces, group_half // pieces, 128), BF16),
            vmem((2, slab_rows, 128), F32),
            vmem((cols, 8, 128), BF16),
            vmem((cols, 8, 128), BF16),
            vmem((2, comps * 8, 128), BF16),
            vmem((2, 4, comps, 128), BF16),
            vmem((2, comps * 8, 128), BF16),
            vmem((2, 4, comps, 128), BF16),
            vmem((4, comps, 128), BF16),
            vmem((2, comps * 8, 128), F32),
            vmem((2, 4, comps, 128), F32),
            vmem((4, comps, 128), F32),
            dma((6,)),
            pltpu.SemaphoreType.REGULAR,
            dma(()),
            dma(()),
            dma((3,)),
            dma((3,)),
            dma((7, GROUPS)),
            dma((rows, GROUPS)),
            dma(()),
            dma(()),
            dma((8,)),
            dma((8,)),
        ],
        compiler_params=pltpu.CompilerParams(
            collective_id=0, has_side_effects=True, vmem_limit_bytes=48 * 2**20
        ),
        name="coupled_apply",
    )(
        *[
            pltpu.with_memory_space_constraint(x, pltpu.HBM)
            for x in (
                wave_field.reshape(comps * 32, 128),
                medium_term.reshape(32, 128),
                node_flux.reshape(comps, 1, nodes),
                node_cell.reshape(1, nodes),
                block_target.reshape(1, cols),
                boundary_matrix,
            )
        ]
    )
    return volume.reshape(wave_field.shape), boundary


def solution(mesh):
    in_specs = (
        P(None, "col", "row", None),
        P("col", "row", None),
        P(None, "col", "row", None),
        P("col", "row", None),
        P("col", "row", None),
        P(None, "row", "col"),
    )
    out_specs = (P(None, "col", "row", None), P(("row", "col"), None))
    return jax.shard_map(
        functools.partial(on_device, mesh.shape["row"], mesh.shape["col"]),
        mesh=mesh,
        in_specs=in_specs,
        out_specs=out_specs,
        check_vma=False,
    )
```

```python
import functools

import jax
import jax.numpy as jnp
from jax import lax
from jax.experimental import pallas as pl
from jax.experimental.pallas import tpu as pltpu
from jax.sharding import PartitionSpec as P

MESH = pl.DeviceIdType.MESH
F32 = jnp.float32
BF16 = jnp.bfloat16
GROUPS = 4


def iota(shape, dim):
    return lax.broadcasted_iota(jnp.int32, shape, dim)


def nt_dot(a, b):
    return lax.dot_general(a, b, (((1,), (1,)), ((), ())), preferred_element_type=F32)


def nn_dot(a, b):
    return lax.dot_general(a, b, (((1,), (0,)), ((), ())), preferred_element_type=F32)


def kernel(
    rows, cols,
    wave_in, medium_in, flux_in, cell_in, target_in, matrix_in,
    volume, boundary_out,
    wave, medium, flux, cell, target, matrix, onehot, picked, order_of, placed, slots, near, outgoing, traces,
    total, parts, landed,
    faces, edges, faces_in, edges_in, corners_in, faces_f, edges_f, corners_f,
    in_sem, ready, near_send, near_recv, pass_send, pass_recv, row_send, row_recv, part_send, part_recv,
    halo_send, halo_recv,
):
    me_r = lax.axis_index("row")
    me_c = lax.axis_index("col")
    comps = wave.shape[0] // 32
    nodes = cell.shape[1]
    slot_len = nodes // cols
    half_slot = slot_len // 2
    span = cols // GROUPS
    mine = me_c // span
    me_n = me_c % span
    after, across, before = [(mine + d) % GROUPS for d in (1, 2, 3)]

    loads = [
        pltpu.make_async_copy(src, dst, in_sem.at[i])
        for i, (src, dst) in enumerate(
            [
                (cell_in, cell),
                (target_in, target),
                (wave_in, wave),
                (flux_in, flux),
                (medium_in, medium),
                (matrix_in, matrix),
            ]
        )
    ]
    for load in loads:
        load.start()

    barrier = pltpu.get_barrier_semaphore()

    def greet(r, c):
        pl.semaphore_signal(barrier, inc=1, device_id=(r, c), device_id_type=MESH)

    greet(me_r, after * span + me_n)
    greet(me_r, before * span + me_n)

    @pl.loop(1, rows)
    def _(i):
        greet((me_r + i) % rows, me_c)

    @pl.loop(1, span)
    def _(i):
        greet(me_r, mine * span + (me_n + i) % span)

    def remote(src, dst, send_sem, recv_sem, r, c):
        return pltpu.make_async_remote_copy(
            src_ref=src,
            dst_ref=dst,
            send_sem=send_sem,
            recv_sem=recv_sem,
            device_id=(r, c),
            device_id_type=MESH,
        )

    loads[0].wait()
    loads[1].wait()
    cells = cell[...]
    place = cells // 128
    onehot[...] = jnp.where(iota((128, nodes), 0) == cells % 128, 1.0, 0.0).astype(BF16)
    node = iota((1, nodes), 1)
    spread = jnp.where(iota((cols, nodes), 0) == iota((cols, nodes), 1) // slot_len, 1.0, 0.0)
    wanted = jnp.broadcast_to(target[...].astype(F32), (8, cols))
    wanted = nn_dot(wanted.astype(BF16), spread.astype(BF16))[:1].astype(jnp.int32)
    within = node % slot_len
    row_of = ((wanted % span) * GROUPS + wanted // span) * 8 + within % half_slot
    lane_half = within // half_slot

    loads[2].wait()
    here = iota((32, nodes), 0) == place

    @pl.loop(0, comps // 8, unroll=2)
    def _(i):
        start = pl.multiple_of(i * 256, 256)
        found = nn_dot(wave[pl.ds(start, 256), :].astype(BF16), onehot[...])
        found = jnp.where(here[None], found.reshape(8, 32, nodes), 0.0)
        found = found.reshape(8, 4, 8, nodes)
        found = (found[:, 0] + found[:, 1]) + (found[:, 2] + found[:, 3])
        picked[pl.ds(pl.multiple_of(i * 64, 64), 64), :] = found.reshape(64, nodes).astype(BF16)

    gather = jnp.where(iota((comps, comps * 8), 0) == iota((comps, comps * 8), 1) // 8, 1.0, 0.0)
    trace = nn_dot(gather.astype(BF16), picked[...])
    blank = jnp.zeros_like(trace)
    sent = None
    for half in range(2):
        match = jnp.logical_and(iota((cols * 8, nodes), 0) == row_of, lane_half == half)
        order = jnp.where(match, 1.0, 0.0).astype(BF16)
        pair = [trace, blank] if half == 0 else [blank, trace]
        term = nt_dot(order, jnp.concatenate(pair, axis=0).astype(BF16))
        sent = term if sent is None else sent + term
    slots[...] = sent.reshape(span, GROUPS, 8, 2 * comps).astype(BF16)

    pl.semaphore_wait(barrier, span - 1 + 2 + rows - 1)

    for group in (after, before):
        pl.semaphore_signal(
            ready, inc=1, device_id=(me_r, group * span + me_n), device_id_type=MESH
        )

    def near_copy(n, source):
        return remote(
            slots.at[n], near.at[:, source], near_send, near_recv, me_r, mine * span + n
        )

    for step in sorted(range(1, span), key=lambda i: -min(i, span - i)):
        near_copy((me_n + step) % span, me_n).start()

    own_slots = pltpu.make_async_copy(slots.at[me_n], near.at[:, me_n], near_recv)
    own_slots.start()

    has = [me_c > 0, me_c < cols - 1, me_r > 0, me_r < rows - 1]
    for side in range(2):
        for x in range(4):
            edges[side, x] = wave[pl.ds(x * 8 + side * 7, comps, stride=32), :].astype(BF16)

    def edge_copy(side):
        return remote(
            edges.at[side],
            edges_in.at[1 - side],
            halo_send.at[2 + side],
            halo_recv.at[2 + side],
            me_r + 2 * side - 1,
            me_c,
        )

    for side in range(2):

        @pl.when(has[2 + side])
        def _():
            edge_copy(side).start()

    for side in range(2):

        @pl.loop(0, comps // 8)
        def _(i):
            rows_of = [wave[pl.ds(i * 256 + j * 32 + side * 24, 8), :] for j in range(8)]
            outer = jnp.concatenate(rows_of, axis=0).astype(BF16)
            faces[side, pl.ds(pl.multiple_of(i * 64, 64), 64), :] = outer

    group_half = span * half_slot
    at_row = iota((2 * group_half, span * 16), 0)
    packed = iota((2 * group_half, span * 16), 1)
    turned_in = packed // (span * 8)
    upper_out = at_row // group_half
    from_node = packed % (span * 8) // 8 * slot_len + packed % 8
    from_node += jnp.where(turned_in == upper_out, 0, half_slot)
    hit = jnp.logical_and(from_node == at_row, packed % 8 < half_slot)
    order_of[...] = jnp.where(hit, 1.0, 0.0).astype(BF16)
    remote(near, near, near_send, near_recv, me_r, after * span + me_n).wait_recv()

    raw = [near[g].reshape(span * 8, 2 * comps) for g in range(GROUPS)]
    turned = [pltpu.roll(block.astype(F32), comps, 1).astype(BF16) for block in raw]
    stacks = [jnp.concatenate(pair, axis=0) for pair in zip(raw, turned)]
    found = nn_dot(order_of[...], jnp.concatenate(stacks, axis=1))
    found = jnp.where(
        iota((group_half, GROUPS * 128), 1) % 128 < comps, found[:group_half], found[group_half:]
    )
    piece = outgoing.shape[1:]
    for g in range(GROUPS):
        outgoing[g] = found[:, g * 128 : g * 128 + 128].reshape(piece).astype(BF16)

    beside = [across, after, before]

    def pass_on(k):
        return remote(
            outgoing.at[beside[k]],
            traces.at[me_r, mine],
            pass_send.at[k],
            pass_recv.at[k],
            me_r,
            beside[k] * span + me_n,
        )

    def passed(k):
        group = [across, before, after][k]
        ref = traces.at[me_r, group]
        return remote(ref, ref, pass_send.at[k], pass_recv.at[k], me_r, group * span + me_n)

    pl.semaphore_wait(ready, 2)
    for k in range(3):
        pass_on(k).start()
    traces[me_r, mine] = outgoing[mine]

    wide = rows // 2

    def row_at(dz, dx):
        return (me_r // wide + dz) % 2 * wide + (me_r % wide + dx) % wide

    across_x = wide // 2
    steps = [(0, across_x), (0, 1), (0, wide - 1), (1, 0)] if wide > 1 else [(1, 0)]
    far_steps = [(1, across_x), (1, 1), (1, wide - 1)] if wide > 1 else []
    plane, opposite = row_at(1, 0), row_at(0, across_x)

    def row_copy(k, step, g, r):
        ref = traces.at[r, g]
        return remote(ref, ref, row_send.at[k, g], row_recv.at[r, g], row_at(*step), me_c)

    def row_arrival(r, g):
        ref = traces.at[r, g]
        return remote(ref, ref, row_send.at[0, g], row_recv.at[r, g], plane, me_c)

    def first_hops(g):
        return [row_copy(k, step, g, me_r) for k, step in enumerate(steps)]

    def second_hops(g, first, last):
        sends = [(4, (0, 1), plane), (5, (0, wide - 1), plane), (6, (1, 0), opposite)]
        return [row_copy(k, step, g, r) for k, step, r in (sends[first:last] if wide > 1 else [])]

    def far_hops(g):
        return [row_copy(4 + k, step, g, me_r) for k, step in enumerate(far_steps)]

    def go(copies):
        for copy in copies:
            copy.start()

    def go_on(g):
        if wide > 1:
            row_arrival(plane, g).wait_recv()
            go(second_hops(g, 0, 2))
            row_arrival(opposite, g).wait_recv()
            go(second_hops(g, 2, 3))

    go(first_hops(mine))

    loads[3].wait()

    @pl.loop(0, comps // 8, unroll=2)
    def _(i):
        start = pl.multiple_of(i * 256, 256)
        wide = jnp.where(here[None], flux[pl.ds(i * 8, 8), :, :], 0.0).reshape(256, nodes)
        upper = wide.astype(BF16)
        lower = (wide - upper.astype(F32)).astype(BF16)
        volume[pl.ds(start, 256), :] = nt_dot(upper, onehot[...]) + nt_dot(lower, onehot[...])

    for k, g in ((1, before), (2, after)):
        passed(k).wait_recv()
        go(far_hops(g))
        go(first_hops(g))

    total[...] = jnp.zeros_like(total)
    go_on(mine)
    passed(0).wait_recv()
    go(far_hops(across))
    go(first_hops(across))

    def face_copy(side):
        return remote(
            faces.at[side],
            faces_in.at[1 - side],
            halo_send.at[side],
            halo_recv.at[side],
            me_r,
            me_c + 2 * side - 1,
        )

    def corner_copy(side, way):
        return remote(
            edges_in.at[side, 3 * way],
            corners_in.at[2 - 2 * way + side],
            halo_send.at[4 + 2 * side + way],
            halo_recv.at[4 + 2 * side + way],
            me_r,
            me_c + 2 * way - 1,
        )

    for side in range(2):

        @pl.when(has[2 + side])
        def _():
            ref = edges_in.at[side]
            remote(
                ref, ref, halo_send.at[3 - side], halo_recv.at[3 - side], me_r + 2 * side - 1, me_c
            ).wait_recv()
            for way in range(2):

                @pl.when(has[way])
                def _():
                    corner_copy(side, way).start()

    loads[5].wait()
    slab = matrix.shape[1]
    third = nodes // 3
    early = mine // 2
    for late in range(2):
        part = (mine // 2 + late) % 2

        def arrivals(step, g):
            row_arrival(row_at(*step), g).wait_recv()

        for step in steps + far_steps:
            if late:
                arrivals(step, across)
                arrivals(step, jnp.where(mine % 2 == 0, before, after))
            else:
                arrivals(step, jnp.where(mine % 2 == 0, after, before))
                if step not in ((1, 0), (0, across_x)) or wide == 1:
                    arrivals(step, mine)

        if not late:
            for side in range(2):

                @pl.when(has[side])
                def _():
                    face_copy(side).start()

        for r in range(rows):
            pieces = []
            for g in range(2):
                block = traces[r, 2 * part + g].astype(F32).reshape(group_half, 2 * comps)
                pieces += [block, pltpu.roll(block, comps, 1)]
            placed[r, pl.ds(pl.multiple_of(part * (nodes // 2), nodes // 2), nodes // 2), :] = (
                jnp.concatenate(pieces, axis=0).astype(BF16)
            )

        if late:
            first, width, joined = (1 - early) * third, 2 * third, 1
        else:
            first, width, joined = 2 * early * third, third, 2

        @pl.loop(0, 2)
        def _(i):
            upright = pl.ds(pl.multiple_of(i * (slab // 2), slab // 2), slab // 2)
            for half in range(2):
                terms = total[half, upright, :]
                for r in range(0, rows, joined):
                    lhs, rhs = [], []
                    for q in range(r, r + joined):
                        columns = pl.ds(pl.multiple_of(q * nodes + first, third), width)
                        lhs.append(matrix[half, upright, columns])
                        rhs.append(placed[q, pl.ds(pl.multiple_of(first, third), width), :])
                    terms += nn_dot(jnp.concatenate(lhs, axis=1), jnp.concatenate(rhs, axis=0))
                total[half, upright, :] = terms

    lower = iota((cols * 8, 128), 1) < comps
    minus = iota((cols * 8, 128), 1) % comps < comps // 2
    folded = []
    for half in range(2):
        tiles = total[half].reshape(cols, 2, 8, 128)
        first, second = [tiles[:, i].reshape(cols * 8, 128) for i in range(2)]
        folded.append(jnp.where(lower, first, pltpu.roll(second, comps, 1)))
    real, imag = folded
    imag = jnp.where(
        minus, -pltpu.roll(imag, 128 - comps // 2, 1), pltpu.roll(imag, comps // 2, 1)
    )
    parts[...] = (real + imag).reshape(cols, 8, 128).astype(BF16)

    def part_copy(t, source):
        return remote(
            parts.at[t], landed.at[source], part_send, part_recv, me_r, t
        )

    for hop in (2, 1, 3, 0):
        first = ((mine + hop) % GROUPS) * span

        @pl.loop(0, span)
        def _(i):
            t = first + i

            @pl.when(t != me_c)
            def _():
                part_copy(t, me_c).start()

    own_part = pltpu.make_async_copy(parts.at[me_c], landed.at[me_c], part_recv)
    own_part.start()

    halos = [
        (faces_in.at[1 - side], faces_f.at[1 - side], side, has[1 - side], (0, 1 - 2 * side))
        for side in range(2)
    ]
    halos += [
        (edges_in.at[side], edges_f.at[side], -1, has[2 + side], None) for side in range(2)
    ]
    halos += [
        (
            corners_in.at[2 - 2 * way + side],
            corners_f.at[2 - 2 * way + side],
            4 + 2 * side + way,
            jnp.logical_and(has[1 - way], has[2 + side]),
            (0, 1 - 2 * way),
        )
        for side in range(2)
        for way in range(2)
    ]
    for got, kept, k, there, step in halos:

        @pl.when(there)
        def _():
            if step is not None:
                remote(
                    got, got, halo_send.at[k], halo_recv.at[k], me_r + step[0], me_c + step[1]
                ).wait_recv()
            kept[...] = got[...].astype(F32)

        @pl.when(jnp.logical_not(there))
        def _():
            kept[...] = jnp.zeros(kept.shape, F32)

    loads[4].wait()
    sublane = iota((8, 128), 0)
    lane = iota((8, 128), 1)

    def depth_sides(v):
        below = jnp.where(lane == 0, 0.0, pltpu.roll(v, 1, 1))
        above = jnp.where(lane == 127, 0.0, pltpu.roll(v, 127, 1))
        return below + above

    def layer(u, low, high):
        below = jnp.where(sublane == 0, jnp.broadcast_to(low, (8, 128)), pltpu.roll(u, 1, 0))
        above = jnp.where(sublane == 7, jnp.broadcast_to(high, (8, 128)), pltpu.roll(u, 7, 0))
        sides = below + above
        outer = depth_sides(sides)
        ring = 2.0 * (sides + depth_sides(u)) + outer
        return u, outer, ring, 4.0 * u + ring

    @pl.loop(0, comps, unroll=4)
    def _(k):
        layers = []
        for x in range(6):
            if x in (0, 5):
                side = 0 if x == 0 else 1
                u = faces_f[side, pl.ds(pl.multiple_of(k * 8, 8), 8), :]
                low = corners_f[2 * side, pl.ds(k, 1), :]
                high = corners_f[2 * side + 1, pl.ds(k, 1), :]
            else:
                u = wave[pl.ds(pl.multiple_of(k * 32 + (x - 1) * 8, 8), 8), :]
                low = edges_f[0, x - 1, pl.ds(k, 1), :]
                high = edges_f[1, x - 1, pl.ds(k, 1), :]
            layers.append(layer(u, low, high))
        for x in range(1, 5):
            u, outer, ring, mass = layers[x]
            stiffness = (8.0 / 3.0) * u - (1.0 / 6.0) * outer
            stiffness -= (1.0 / 12.0) * (layers[x - 1][2] + layers[x + 1][2])
            mass_sum = (2.0 * mass + (layers[x - 1][3] + layers[x + 1][3])) * (1.0 / 27.0)
            where = pl.ds(pl.multiple_of(k * 32 + (x - 1) * 8, 8), 8)
            volume[where, :] = (
                stiffness - medium[pl.ds((x - 1) * 8, 8), :] * mass_sum - volume[where, :]
            )

    if span > 1:
        others = slots.at[pl.ds(0, span - 1)]
        remote(others, others, near_send, near_recv, me_r, after * span + me_n).wait_send()

    for k in range(3):
        pass_on(k).wait_send()

    for g in (mine, before, after, across):
        for copy in first_hops(g):
            copy.wait_send()
    for copy in second_hops(mine, 0, 3):
        copy.wait_send()
    for g in (before, after, across):
        for copy in far_hops(g):
            copy.wait_send()

    for side in range(2):

        @pl.when(has[side])
        def _():
            face_copy(side).wait_send()

        @pl.when(has[2 + side])
        def _():
            edge_copy(side).wait_send()
            for way in range(2):

                @pl.when(has[way])
                def _():
                    corner_copy(side, way).wait_send()

    remote(landed, landed, part_send, part_recv, me_r, after * span + me_n).wait_recv()

    sums = jnp.sum(landed[...].astype(F32), axis=0)
    boundary_out[0:8, :] = sums[:, :comps]
    boundary_out[8:16, :] = pltpu.roll(sums, comps, 1)[:, :comps]

    others = parts.at[pl.ds(0, cols - 1)]
    remote(others, others, part_send, part_recv, me_r, after * span + me_n).wait_send()


def on_device(rows, cols, wave_field, medium_term, node_flux, node_cell, block_target, boundary_matrix):
    comps = wave_field.shape[0]
    nodes = node_cell.shape[-1]
    slab_rows, width = boundary_matrix.shape[1:]
    own_rows = slab_rows // cols
    group_half = nodes // GROUPS // 2
    pieces = 6 if group_half % 48 == 0 else 2
    vmem = pltpu.VMEM
    dma = pltpu.SemaphoreType.DMA
    volume, boundary = pl.pallas_call(
        functools.partial(kernel, rows, cols),
        out_shape=(
            pltpu.VMEM((comps * 32, 128), F32),
            pltpu.VMEM((own_rows, comps), F32),
        ),
        in_specs=[pl.BlockSpec(memory_space=pltpu.HBM)] * 6,
        out_specs=(pl.BlockSpec(memory_space=pltpu.VMEM), pl.BlockSpec(memory_space=pltpu.VMEM)),
        scratch_shapes=[
            vmem((comps * 32, 128), F32),
            vmem((32, 128), F32),
            vmem((comps, 1, nodes), F32),
            vmem((1, nodes), jnp.int32),
            vmem((1, cols), jnp.int32),
            vmem((2, slab_rows, width), BF16),
            vmem((128, nodes), BF16),
            vmem((comps * 8, nodes), BF16),
            vmem((nodes // GROUPS, cols // GROUPS * 16), BF16),
            vmem((rows, nodes, 128), BF16),
            vmem((cols // GROUPS, GROUPS, 8, 128), BF16),
            vmem((GROUPS, cols // GROUPS, 8, 128), BF16),
            vmem((GROUPS, pieces, group_half // pieces, 128), BF16),
            vmem((rows, GROUPS, pieces, group_half // pieces, 128), BF16),
            vmem((2, slab_rows, 128), F32),
            vmem((cols, 8, 128), BF16),
            vmem((cols, 8, 128), BF16),
            vmem((2, comps * 8, 128), BF16),
            vmem((2, 4, comps, 128), BF16),
            vmem((2, comps * 8, 128), BF16),
            vmem((2, 4, comps, 128), BF16),
            vmem((4, comps, 128), BF16),
            vmem((2, comps * 8, 128), F32),
            vmem((2, 4, comps, 128), F32),
            vmem((4, comps, 128), F32),
            dma((6,)),
            pltpu.SemaphoreType.REGULAR,
            dma(()),
            dma(()),
            dma((3,)),
            dma((3,)),
            dma((7, GROUPS)),
            dma((rows, GROUPS)),
            dma(()),
            dma(()),
            dma((8,)),
            dma((8,)),
        ],
        compiler_params=pltpu.CompilerParams(
            collective_id=0, has_side_effects=True, vmem_limit_bytes=48 * 2**20
        ),
        name="coupled_apply",
    )(
        *[
            pltpu.with_memory_space_constraint(x, pltpu.HBM)
            for x in (
                wave_field.reshape(comps * 32, 128),
                medium_term.reshape(32, 128),
                node_flux.reshape(comps, 1, nodes),
                node_cell.reshape(1, nodes),
                block_target.reshape(1, cols),
                boundary_matrix,
            )
        ]
    )
    return volume.reshape(wave_field.shape), boundary


def solution(mesh):
    in_specs = (
        P(None, "col", "row", None),
        P("col", "row", None),
        P(None, "col", "row", None),
        P("col", "row", None),
        P("col", "row", None),
        P(None, "row", "col"),
    )
    out_specs = (P(None, "col", "row", None), P(("row", "col"), None))
    return jax.shard_map(
        functools.partial(on_device, mesh.shape["row"], mesh.shape["col"]),
        mesh=mesh,
        in_specs=in_specs,
        out_specs=out_specs,
        check_vma=False,
    )
```

```python
import functools

import jax
import jax.numpy as jnp
from jax import lax
from jax.experimental import pallas as pl
from jax.experimental.pallas import tpu as pltpu
from jax.sharding import PartitionSpec as P

MESH = pl.DeviceIdType.MESH
F32 = jnp.float32
BF16 = jnp.bfloat16
GROUPS = 4


def iota(shape, dim):
    return lax.broadcasted_iota(jnp.int32, shape, dim)


def nt_dot(a, b):
    return lax.dot_general(a, b, (((1,), (1,)), ((), ())), preferred_element_type=F32)


def nn_dot(a, b):
    return lax.dot_general(a, b, (((1,), (0,)), ((), ())), preferred_element_type=F32)


def kernel(
    rows, cols,
    wave_in, medium_in, flux_in, cell_in, target_in, matrix_in,
    volume, boundary_out,
    wave, medium, flux, cell, target, matrix, onehot, picked, order_of, placed, slots, near, outgoing, traces,
    total, parts, landed,
    faces, edges, faces_in, edges_in, corners_in, faces_f, edges_f, corners_f,
    in_sem, ready, near_send, near_recv, pass_send, pass_recv, row_send, row_recv, part_send, part_recv,
    halo_send, halo_recv,
):
    me_r = lax.axis_index("row")
    me_c = lax.axis_index("col")
    comps = wave.shape[0] // 32
    nodes = cell.shape[1]
    slot_len = nodes // cols
    half_slot = slot_len // 2
    span = cols // GROUPS
    mine = me_c // span
    me_n = me_c % span
    after, across, before = [(mine + d) % GROUPS for d in (1, 2, 3)]

    loads = [
        pltpu.make_async_copy(src, dst, in_sem.at[i])
        for i, (src, dst) in enumerate(
            [
                (cell_in, cell),
                (target_in, target),
                (wave_in, wave),
                (flux_in, flux),
                (medium_in, medium),
                (matrix_in, matrix),
            ]
        )
    ]
    for load in loads:
        load.start()

    barrier = pltpu.get_barrier_semaphore()

    def greet(r, c):
        pl.semaphore_signal(barrier, inc=1, device_id=(r, c), device_id_type=MESH)

    greet(me_r, after * span + me_n)
    greet(me_r, before * span + me_n)

    @pl.loop(1, rows)
    def _(i):
        greet((me_r + i) % rows, me_c)

    @pl.loop(1, span)
    def _(i):
        greet(me_r, mine * span + (me_n + i) % span)

    def remote(src, dst, send_sem, recv_sem, r, c):
        return pltpu.make_async_remote_copy(
            src_ref=src,
            dst_ref=dst,
            send_sem=send_sem,
            recv_sem=recv_sem,
            device_id=(r, c),
            device_id_type=MESH,
        )

    loads[0].wait()
    loads[1].wait()
    cells = cell[...]
    place = cells // 128
    onehot[...] = jnp.where(iota((128, nodes), 0) == cells % 128, 1.0, 0.0).astype(BF16)
    node = iota((1, nodes), 1)
    spread = jnp.where(iota((cols, nodes), 0) == iota((cols, nodes), 1) // slot_len, 1.0, 0.0)
    wanted = jnp.broadcast_to(target[...].astype(F32), (8, cols))
    wanted = nn_dot(wanted.astype(BF16), spread.astype(BF16))[:1].astype(jnp.int32)
    within = node % slot_len
    row_of = ((wanted % span) * GROUPS + wanted // span) * 8 + within % half_slot
    lane_half = within // half_slot

    loads[2].wait()
    here = iota((32, nodes), 0) == place

    @pl.loop(0, comps // 8, unroll=2)
    def _(i):
        start = pl.multiple_of(i * 256, 256)
        found = nn_dot(wave[pl.ds(start, 256), :].astype(BF16), onehot[...])
        found = jnp.where(here[None], found.reshape(8, 32, nodes), 0.0)
        found = found.reshape(8, 4, 8, nodes)
        found = (found[:, 0] + found[:, 1]) + (found[:, 2] + found[:, 3])
        picked[pl.ds(pl.multiple_of(i * 64, 64), 64), :] = found.reshape(64, nodes).astype(BF16)

    gather = jnp.where(iota((comps, comps * 8), 0) == iota((comps, comps * 8), 1) // 8, 1.0, 0.0)
    trace = nn_dot(gather.astype(BF16), picked[...])
    blank = jnp.zeros_like(trace)
    sent = None
    for half in range(2):
        match = jnp.logical_and(iota((cols * 8, nodes), 0) == row_of, lane_half == half)
        order = jnp.where(match, 1.0, 0.0).astype(BF16)
        pair = [trace, blank] if half == 0 else [blank, trace]
        term = nt_dot(order, jnp.concatenate(pair, axis=0).astype(BF16))
        sent = term if sent is None else sent + term
    slots[...] = sent.reshape(span, GROUPS, 8, 2 * comps).astype(BF16)

    pl.semaphore_wait(barrier, span - 1 + 2 + rows - 1)

    for group in (after, before):
        pl.semaphore_signal(
            ready, inc=1, device_id=(me_r, group * span + me_n), device_id_type=MESH
        )

    def near_copy(n, source):
        return remote(
            slots.at[n], near.at[:, source], near_send, near_recv, me_r, mine * span + n
        )

    for step in sorted(range(1, span), key=lambda i: -min(i, span - i)):
        near_copy((me_n + step) % span, me_n).start()

    own_slots = pltpu.make_async_copy(slots.at[me_n], near.at[:, me_n], near_recv)
    own_slots.start()

    has = [me_c > 0, me_c < cols - 1, me_r > 0, me_r < rows - 1]
    for side in range(2):
        for x in range(4):
            edges[side, x] = wave[pl.ds(x * 8 + side * 7, comps, stride=32), :].astype(BF16)

    def edge_copy(side):
        return remote(
            edges.at[side],
            edges_in.at[1 - side],
            halo_send.at[2 + side],
            halo_recv.at[2 + side],
            me_r + 2 * side - 1,
            me_c,
        )

    for side in range(2):

        @pl.when(has[2 + side])
        def _():
            edge_copy(side).start()

    for side in range(2):

        @pl.loop(0, comps // 8)
        def _(i):
            rows_of = [wave[pl.ds(i * 256 + j * 32 + side * 24, 8), :] for j in range(8)]
            outer = jnp.concatenate(rows_of, axis=0).astype(BF16)
            faces[side, pl.ds(pl.multiple_of(i * 64, 64), 64), :] = outer

    group_half = span * half_slot
    at_row = iota((2 * group_half, span * 16), 0)
    packed = iota((2 * group_half, span * 16), 1)
    turned_in = packed // (span * 8)
    upper_out = at_row // group_half
    from_node = packed % (span * 8) // 8 * slot_len + packed % 8
    from_node += jnp.where(turned_in == upper_out, 0, half_slot)
    hit = jnp.logical_and(from_node == at_row, packed % 8 < half_slot)
    order_of[...] = jnp.where(hit, 1.0, 0.0).astype(BF16)
    remote(near, near, near_send, near_recv, me_r, after * span + me_n).wait_recv()

    raw = [near[g].reshape(span * 8, 2 * comps) for g in range(GROUPS)]
    turned = [pltpu.roll(block.astype(F32), comps, 1).astype(BF16) for block in raw]
    stacks = [jnp.concatenate(pair, axis=0) for pair in zip(raw, turned)]
    found = nn_dot(order_of[...], jnp.concatenate(stacks, axis=1))
    found = jnp.where(
        iota((group_half, GROUPS * 128), 1) % 128 < comps, found[:group_half], found[group_half:]
    )
    piece = outgoing.shape[1:]
    for g in range(GROUPS):
        outgoing[g] = found[:, g * 128 : g * 128 + 128].reshape(piece).astype(BF16)

    beside = [across, after, before]

    def pass_on(k):
        return remote(
            outgoing.at[beside[k]],
            traces.at[me_r, mine],
            pass_send.at[k],
            pass_recv.at[k],
            me_r,
            beside[k] * span + me_n,
        )

    def passed(k):
        group = [across, before, after][k]
        ref = traces.at[me_r, group]
        return remote(ref, ref, pass_send.at[k], pass_recv.at[k], me_r, group * span + me_n)

    pl.semaphore_wait(ready, 2)
    for k in range(3):
        pass_on(k).start()
    traces[me_r, mine] = outgoing[mine]

    wide = rows // 2

    def row_at(dz, dx):
        return (me_r // wide + dz) % 2 * wide + (me_r % wide + dx) % wide

    across_x = wide // 2
    steps = [(0, across_x), (0, 1), (0, wide - 1), (1, 0)] if wide > 1 else [(1, 0)]
    far_steps = [(1, across_x), (1, 1), (1, wide - 1)] if wide > 1 else []
    plane, opposite = row_at(1, 0), row_at(0, across_x)

    def row_copy(k, step, g, r):
        ref = traces.at[r, g]
        return remote(ref, ref, row_send.at[k, g], row_recv.at[r, g], row_at(*step), me_c)

    def row_arrival(r, g):
        ref = traces.at[r, g]
        return remote(ref, ref, row_send.at[0, g], row_recv.at[r, g], plane, me_c)

    def first_hops(g):
        return [row_copy(k, step, g, me_r) for k, step in enumerate(steps)]

    def second_hops(g, first, last):
        sends = [(4, (0, 1), plane), (5, (0, wide - 1), plane), (6, (1, 0), opposite)]
        return [row_copy(k, step, g, r) for k, step, r in (sends[first:last] if wide > 1 else [])]

    def far_hops(g):
        return [row_copy(4 + k, step, g, me_r) for k, step in enumerate(far_steps)]

    def go(copies):
        for copy in copies:
            copy.start()

    def go_on(g):
        if wide > 1:
            row_arrival(plane, g).wait_recv()
            go(second_hops(g, 0, 2))
            row_arrival(opposite, g).wait_recv()
            go(second_hops(g, 2, 3))

    go(first_hops(mine))

    loads[3].wait()

    @pl.loop(0, comps // 8, unroll=2)
    def _(i):
        start = pl.multiple_of(i * 256, 256)
        wide = jnp.where(here[None], flux[pl.ds(i * 8, 8), :, :], 0.0).reshape(256, nodes)
        upper = wide.astype(BF16)
        lower = (wide - upper.astype(F32)).astype(BF16)
        volume[pl.ds(start, 256), :] = nt_dot(upper, onehot[...]) + nt_dot(lower, onehot[...])

    for k, g in ((1, before), (2, after)):
        passed(k).wait_recv()
        go(far_hops(g))
        go(first_hops(g))

    total[...] = jnp.zeros_like(total)
    go_on(mine)
    passed(0).wait_recv()
    go(far_hops(across))
    go(first_hops(across))

    def face_copy(side):
        return remote(
            faces.at[side],
            faces_in.at[1 - side],
            halo_send.at[side],
            halo_recv.at[side],
            me_r,
            me_c + 2 * side - 1,
        )

    def corner_copy(side, way):
        return remote(
            edges_in.at[side, 3 * way],
            corners_in.at[2 - 2 * way + side],
            halo_send.at[4 + 2 * side + way],
            halo_recv.at[4 + 2 * side + way],
            me_r,
            me_c + 2 * way - 1,
        )

    for side in range(2):

        @pl.when(has[2 + side])
        def _():
            ref = edges_in.at[side]
            remote(
                ref, ref, halo_send.at[3 - side], halo_recv.at[3 - side], me_r + 2 * side - 1, me_c
            ).wait_recv()
            for way in range(2):

                @pl.when(has[way])
                def _():
                    corner_copy(side, way).start()

    loads[5].wait()
    slab = matrix.shape[1]
    third = nodes // 3
    early = mine // 2
    for late in range(2):
        part = (mine // 2 + late) % 2

        def arrivals(step, g):
            row_arrival(row_at(*step), g).wait_recv()

        for step in steps + far_steps:
            if late:
                arrivals(step, across)
                arrivals(step, jnp.where(mine % 2 == 0, before, after))
            else:
                arrivals(step, jnp.where(mine % 2 == 0, after, before))
                if step not in ((1, 0), (0, across_x)) or wide == 1:
                    arrivals(step, mine)

        if not late:
            for side in range(2):

                @pl.when(has[side])
                def _():
                    face_copy(side).start()

        for r in range(rows):
            pieces = []
            for g in range(2):
                block = traces[r, 2 * part + g].astype(F32).reshape(group_half, 2 * comps)
                pieces += [block, pltpu.roll(block, comps, 1)]
            placed[r, pl.ds(pl.multiple_of(part * (nodes // 2), nodes // 2), nodes // 2), :] = (
                jnp.concatenate(pieces, axis=0).astype(BF16)
            )

        if late:
            first, width, joined = (1 - early) * third, 2 * third, 1
        else:
            first, width, joined = 2 * early * third, third, 2

        @pl.loop(0, 2)
        def _(i):
            upright = pl.ds(pl.multiple_of(i * (slab // 2), slab // 2), slab // 2)
            for half in range(2):
                terms = total[half, upright, :]
                for r in range(0, rows, joined):
                    lhs, rhs = [], []
                    for q in range(r, r + joined):
                        columns = pl.ds(pl.multiple_of(q * nodes + first, third), width)
                        lhs.append(matrix[half, upright, columns])
                        rhs.append(placed[q, pl.ds(pl.multiple_of(first, third), width), :])
                    terms += nn_dot(jnp.concatenate(lhs, axis=1), jnp.concatenate(rhs, axis=0))
                total[half, upright, :] = terms

    lower = iota((cols * 8, 128), 1) < comps
    minus = iota((cols * 8, 128), 1) % comps < comps // 2
    folded = []
    for half in range(2):
        tiles = total[half].reshape(cols, 2, 8, 128)
        first, second = [tiles[:, i].reshape(cols * 8, 128) for i in range(2)]
        folded.append(jnp.where(lower, first, pltpu.roll(second, comps, 1)))
    real, imag = folded
    imag = jnp.where(
        minus, -pltpu.roll(imag, 128 - comps // 2, 1), pltpu.roll(imag, comps // 2, 1)
    )
    parts[...] = (real + imag).reshape(cols, 8, 128).astype(BF16)

    def part_copy(t, source):
        return remote(
            parts.at[t], landed.at[source], part_send, part_recv, me_r, t
        )

    for hop in (2, 1, 3, 0):
        first = ((mine + hop) % GROUPS) * span

        @pl.loop(0, span)
        def _(i):
            t = first + (me_n + span // 2 + i) % span

            @pl.when(t != me_c)
            def _():
                part_copy(t, me_c).start()

    own_part = pltpu.make_async_copy(parts.at[me_c], landed.at[me_c], part_recv)
    own_part.start()

    halos = [
        (faces_in.at[1 - side], faces_f.at[1 - side], side, has[1 - side], (0, 1 - 2 * side))
        for side in range(2)
    ]
    halos += [
        (edges_in.at[side], edges_f.at[side], -1, has[2 + side], None) for side in range(2)
    ]
    halos += [
        (
            corners_in.at[2 - 2 * way + side],
            corners_f.at[2 - 2 * way + side],
            4 + 2 * side + way,
            jnp.logical_and(has[1 - way], has[2 + side]),
            (0, 1 - 2 * way),
        )
        for side in range(2)
        for way in range(2)
    ]
    for got, kept, k, there, step in halos:

        @pl.when(there)
        def _():
            if step is not None:
                remote(
                    got, got, halo_send.at[k], halo_recv.at[k], me_r + step[0], me_c + step[1]
                ).wait_recv()
            kept[...] = got[...].astype(F32)

        @pl.when(jnp.logical_not(there))
        def _():
            kept[...] = jnp.zeros(kept.shape, F32)

    loads[4].wait()
    sublane = iota((8, 128), 0)
    lane = iota((8, 128), 1)

    def depth_sides(v):
        below = jnp.where(lane == 0, 0.0, pltpu.roll(v, 1, 1))
        above = jnp.where(lane == 127, 0.0, pltpu.roll(v, 127, 1))
        return below + above

    def layer(u, low, high):
        below = jnp.where(sublane == 0, jnp.broadcast_to(low, (8, 128)), pltpu.roll(u, 1, 0))
        above = jnp.where(sublane == 7, jnp.broadcast_to(high, (8, 128)), pltpu.roll(u, 7, 0))
        sides = below + above
        outer = depth_sides(sides)
        ring = 2.0 * (sides + depth_sides(u)) + outer
        return u, outer, ring, 4.0 * u + ring

    @pl.loop(0, comps, unroll=8)
    def _(k):
        layers = []
        for x in range(6):
            if x in (0, 5):
                side = 0 if x == 0 else 1
                u = faces_f[side, pl.ds(pl.multiple_of(k * 8, 8), 8), :]
                low = corners_f[2 * side, pl.ds(k, 1), :]
                high = corners_f[2 * side + 1, pl.ds(k, 1), :]
            else:
                u = wave[pl.ds(pl.multiple_of(k * 32 + (x - 1) * 8, 8), 8), :]
                low = edges_f[0, x - 1, pl.ds(k, 1), :]
                high = edges_f[1, x - 1, pl.ds(k, 1), :]
            layers.append(layer(u, low, high))
        for x in range(1, 5):
            u, outer, ring, mass = layers[x]
            stiffness = (8.0 / 3.0) * u - (1.0 / 6.0) * outer
            stiffness -= (1.0 / 12.0) * (layers[x - 1][2] + layers[x + 1][2])
            mass_sum = (2.0 * mass + (layers[x - 1][3] + layers[x + 1][3])) * (1.0 / 27.0)
            where = pl.ds(pl.multiple_of(k * 32 + (x - 1) * 8, 8), 8)
            volume[where, :] = (
                stiffness - medium[pl.ds((x - 1) * 8, 8), :] * mass_sum - volume[where, :]
            )

    if span > 1:
        others = slots.at[pl.ds(0, span - 1)]
        remote(others, others, near_send, near_recv, me_r, after * span + me_n).wait_send()

    for k in range(3):
        pass_on(k).wait_send()

    for g in (mine, before, after, across):
        for copy in first_hops(g):
            copy.wait_send()
    for copy in second_hops(mine, 0, 3):
        copy.wait_send()
    for g in (before, after, across):
        for copy in far_hops(g):
            copy.wait_send()

    for side in range(2):

        @pl.when(has[side])
        def _():
            face_copy(side).wait_send()

        @pl.when(has[2 + side])
        def _():
            edge_copy(side).wait_send()
            for way in range(2):

                @pl.when(has[way])
                def _():
                    corner_copy(side, way).wait_send()

    remote(landed, landed, part_send, part_recv, me_r, after * span + me_n).wait_recv()

    sums = jnp.sum(landed[...].astype(F32), axis=0)
    boundary_out[0:8, :] = sums[:, :comps]
    boundary_out[8:16, :] = pltpu.roll(sums, comps, 1)[:, :comps]

    others = parts.at[pl.ds(0, cols - 1)]
    remote(others, others, part_send, part_recv, me_r, after * span + me_n).wait_send()


def on_device(rows, cols, wave_field, medium_term, node_flux, node_cell, block_target, boundary_matrix):
    comps = wave_field.shape[0]
    nodes = node_cell.shape[-1]
    slab_rows, width = boundary_matrix.shape[1:]
    own_rows = slab_rows // cols
    group_half = nodes // GROUPS // 2
    pieces = 6 if group_half % 48 == 0 else 2
    vmem = pltpu.VMEM
    dma = pltpu.SemaphoreType.DMA
    volume, boundary = pl.pallas_call(
        functools.partial(kernel, rows, cols),
        out_shape=(
            pltpu.VMEM((comps * 32, 128), F32),
            pltpu.VMEM((own_rows, comps), F32),
        ),
        in_specs=[pl.BlockSpec(memory_space=pltpu.HBM)] * 6,
        out_specs=(pl.BlockSpec(memory_space=pltpu.VMEM), pl.BlockSpec(memory_space=pltpu.VMEM)),
        scratch_shapes=[
            vmem((comps * 32, 128), F32),
            vmem((32, 128), F32),
            vmem((comps, 1, nodes), F32),
            vmem((1, nodes), jnp.int32),
            vmem((1, cols), jnp.int32),
            vmem((2, slab_rows, width), BF16),
            vmem((128, nodes), BF16),
            vmem((comps * 8, nodes), BF16),
            vmem((nodes // GROUPS, cols // GROUPS * 16), BF16),
            vmem((rows, nodes, 128), BF16),
            vmem((cols // GROUPS, GROUPS, 8, 128), BF16),
            vmem((GROUPS, cols // GROUPS, 8, 128), BF16),
            vmem((GROUPS, pieces, group_half // pieces, 128), BF16),
            vmem((rows, GROUPS, pieces, group_half // pieces, 128), BF16),
            vmem((2, slab_rows, 128), F32),
            vmem((cols, 8, 128), BF16),
            vmem((cols, 8, 128), BF16),
            vmem((2, comps * 8, 128), BF16),
            vmem((2, 4, comps, 128), BF16),
            vmem((2, comps * 8, 128), BF16),
            vmem((2, 4, comps, 128), BF16),
            vmem((4, comps, 128), BF16),
            vmem((2, comps * 8, 128), F32),
            vmem((2, 4, comps, 128), F32),
            vmem((4, comps, 128), F32),
            dma((6,)),
            pltpu.SemaphoreType.REGULAR,
            dma(()),
            dma(()),
            dma((3,)),
            dma((3,)),
            dma((7, GROUPS)),
            dma((rows, GROUPS)),
            dma(()),
            dma(()),
            dma((8,)),
            dma((8,)),
        ],
        compiler_params=pltpu.CompilerParams(
            collective_id=0, has_side_effects=True, vmem_limit_bytes=48 * 2**20
        ),
        name="coupled_apply",
    )(
        *[
            pltpu.with_memory_space_constraint(x, pltpu.HBM)
            for x in (
                wave_field.reshape(comps * 32, 128),
                medium_term.reshape(32, 128),
                node_flux.reshape(comps, 1, nodes),
                node_cell.reshape(1, nodes),
                block_target.reshape(1, cols),
                boundary_matrix,
            )
        ]
    )
    return volume.reshape(wave_field.shape), boundary


def solution(mesh):
    in_specs = (
        P(None, "col", "row", None),
        P("col", "row", None),
        P(None, "col", "row", None),
        P("col", "row", None),
        P("col", "row", None),
        P(None, "row", "col"),
    )
    out_specs = (P(None, "col", "row", None), P(("row", "col"), None))
    return jax.shard_map(
        functools.partial(on_device, mesh.shape["row"], mesh.shape["col"]),
        mesh=mesh,
        in_specs=in_specs,
        out_specs=out_specs,
        check_vma=False,
    )
```
